32 devices in a mesh: dp: 8 (over y, x, core), mp: 4 (over z).
Axes of the slice: x: 2, y: 2, z: 4, core: 2. Of those that a mesh axis runs over, the one named last changes fastest.
Arguments:
- inputs: bfloat16 [8192, 2048], P('dp'), may hold values from -6 to 6
- segments: int32 [8192], P('dp'), may hold values from 0 to 511, as said below
- padding: int32 [8192], P('dp'), may hold values from 0 to 1, as said below
- first_gain: bfloat16 [2048], P('dp'), may hold values from 0.5 to 1.5
- first_shift: bfloat16 [2048], P('dp'), may hold values from -4 to 4
- second_gain: bfloat16 [2048], P('dp'), may hold values from 0.5 to 1.5
- second_shift: bfloat16 [2048], P('dp'), may hold values from -4 to 4
- joint_weight: bfloat16 [2048, 6144], P('dp', 'mp'), may hold values from -1 to 1
- joint_bias: bfloat16 [6144], P(('mp', 'dp')), may hold values from -4 to 4
- dense_weight: bfloat16 [2048, 2048], P('mp', 'dp'), may hold values from -0.75 to 0.75
- dense_bias: bfloat16 [2048], P('dp'), may hold values from -4 to 4
- expand_weight: bfloat16 [2048, 8192], P('dp', 'mp'), may hold values from -0.125 to 0.125
- expand_bias: bfloat16 [8192], P(('mp', 'dp')), may hold values from -6 to 6
- reduce_weight: bfloat16 [8192, 2048], P('mp', 'dp'), may hold values from -0.0625 to 0.0625
- reduce_bias: bfloat16 [2048], P('dp'), may hold values from -4 to 4
- cotangent: bfloat16 [8192, 2048], P('dp'), may hold values from -6 to 6
Outputs:
- result: bfloat16 [8192, 2048], P('dp')
- inputs_back: bfloat16 [8192, 2048], P('dp')
- first_gain_back: float32 [2048], P('dp')
- first_shift_back: float32 [2048], P('dp')
- second_gain_back: float32 [2048], P('dp')
- second_shift_back: float32 [2048], P('dp')
- joint_weight_back: float32 [2048, 6144], P('dp', 'mp')
- joint_bias_back: float32 [6144], P(('mp', 'dp'))
- dense_weight_back: float32 [2048, 2048], P('mp', 'dp')
- dense_bias_back: float32 [2048], P('dp')
- expand_weight_back: float32 [2048, 8192], P('dp', 'mp')
- expand_bias_back: float32 [8192], P(('mp', 'dp'))
- reduce_weight_back: float32 [8192, 2048], P('mp', 'dp')
- reduce_bias_back: float32 [2048], P('dp')
The draws below stay inside these ranges and needn't reach their ends.
Inputs may be any that keep to these rules, and one draw needn't show every extreme that they name: `segments`: within each aligned block of 512 rows the ids never fall from row to row; a block ends with 1 to 384 padding rows that carry the id 512 - 1, and its sequences carry smaller ids; no sequence crosses a block's end. 0 exactly on the padding rows that end each block of 512 rows.
All inputs are finite; a program needn't handle non-finite values.
Results may differ from the reference program's by a relative error of at most 0.018.
Values may be sent and summed in bfloat16 or wider, within the bound.
No kernel may reach another device: no remote copies, remote signals or barrier semaphores. Data moves between devices by JAX's collectives and lax.ppermute only.
A program may use at most 256 MiB of HBM per device.

```python
import math
import jax
import jax.numpy as jnp
from jax import lax

D = 2048
H = 8
HD = 256
ROT = 64
FF = 8192
ROWS = 512
TOKENS = 8192
N_MP = 4


def block_layout(key):
    base = jax.random.fold_in(key, 29)
    pad_key, start_key = jax.random.split(base)
    block_count = TOKENS // ROWS
    padded = jax.random.randint(pad_key, (block_count, 1), 1, 3 * ROWS // 4 + 1)
    indices = jnp.arange(ROWS, dtype=jnp.int32)[None, :]
    filled = indices < ROWS - padded
    starts = (jax.random.randint(start_key, (block_count, ROWS), 0, max(ROWS // 4, 2)) == 0) & (indices > 0)
    labels = jnp.cumsum(starts.astype(jnp.int32), axis=1)
    labels = jnp.where(filled, labels, ROWS - 1)
    return (labels.reshape(TOKENS).astype(jnp.int32), filled.astype(jnp.int32).reshape(TOKENS))


def draw_segments(key, part):
    labels, filled = block_layout(key)
    return labels


def draw_padding(key, part):
    labels, filled = block_layout(key)
    return filled


def draw_joint_weight(key, part):
    base = jax.random.fold_in(key, 17)
    drawn_key = jax.random.fold_in(base, 0)
    drawn = jnp.clip(jax.random.normal(drawn_key, (D, H, 3, HD), jnp.float32), -6.0, 6.0) * D ** (-0.5)
    return jnp.clip(drawn.reshape(D, 3 * D), -1.0, 1.0).astype(jnp.bfloat16)


def strengthened(array, key, source, target, shards_of, factor):
    def block_of(position):
        return (jnp.arange(array.shape[position]) // (array.shape[position] // shards_of)).reshape((-1,) + (1,) * (array.ndim - 1 - position))

    near = jax.random.permutation(key, shards_of)[block_of(target)]
    far = (block_of(target) + shards_of // 2) % shards_of
    return jnp.where((block_of(source) == near) | (block_of(source) == far), factor * array, array)


def levels(own_key, extent, cuts, low, largest):
    level, own = 1.0, jax.random.fold_in(own_key, 6)
    for axis_at, blocks in cuts:
        heights = jnp.exp(jax.random.uniform(jax.random.fold_in(own, axis_at), (blocks,), jnp.float32, low / len(cuts), largest / len(cuts)))
        level = level * jnp.repeat(heights, extent[axis_at] // blocks).reshape([-1 if axis == axis_at else 1 for axis in range(len(extent))])
    return level


def scatter_about(key, shape, spread, reach, shards=(), kind=jnp.bfloat16):
    array = jax.random.normal(key, shape, jnp.float32) * spread
    if len(shards) > 0:
        array = levels(key, shape, shards, -0.22, 0.18) * array
    return jnp.clip(array, min=-reach, max=reach).astype(kind)


def gaussian_with(own_key, dims, spread, most, shards, heavy, kind=jnp.bfloat16):
    values = spread * jax.random.normal(own_key, dims, jnp.float32)
    if shards:
        values = values * levels(own_key, dims, shards, -0.22, 0.18)
    return jnp.clip(strengthened(values, jax.random.fold_in(own_key, 3), *heavy), -most, most).astype(kind)


def setup_inputs(seed: int = 0) -> dict:
    seeds = jax.random.split(jax.random.key(seed), 17)
    inputs = gaussian_with(seeds[0], (TOKENS, D), 1.0, 6.0, ((0, 8),), (0, 1, 8, 2.0))
    segments = draw_segments(jax.random.fold_in(seeds[16], 71), 0)
    padding = draw_padding(jax.random.fold_in(seeds[16], 71), 0)
    first_gain = jnp.clip(1.0 + 0.1 * jax.random.normal(seeds[3], (D,), jnp.float32), 0.5, 1.5).astype(jnp.bfloat16)
    first_shift = scatter_about(seeds[4], (D,), 0.3, 4.0, ((0, 8),))
    second_gain = jnp.clip(1.0 + 0.1 * jax.random.normal(seeds[5], (D,), jnp.float32), 0.5, 1.5).astype(jnp.bfloat16)
    second_shift = scatter_about(seeds[6], (D,), 0.3, 4.0, ((0, 8),))
    joint_weight = draw_joint_weight(jax.random.fold_in(seeds[16], 71), 0)
    joint_bias = scatter_about(seeds[8], (3 * D,), 0.3, 4.0, ((0, 32),))
    dense_weight = scatter_about(seeds[9], (D, D), (D * 16 // ROWS) ** -0.5, 0.75, ((0, 4), (1, 8)))
    dense_bias = scatter_about(seeds[10], (D,), 0.3, 4.0, ((0, 8),))
    expand_weight = scatter_about(seeds[11], (D, FF), D ** -0.5, 0.125, ((0, 8), (1, 4)))
    expand_bias = scatter_about(seeds[12], (FF,), 0.5, 6.0, ((0, 32),))
    reduce_weight = scatter_about(seeds[13], (FF, D), FF ** -0.5, 0.0625, ((0, 4), (1, 8)))
    reduce_bias = scatter_about(seeds[14], (D,), 0.3, 4.0, ((0, 8),))
    cotangent = gaussian_with(seeds[15], (TOKENS, D), 1.0, 6.0, ((0, 8),), (0, 1, 8, 2.0))
    return dict(inputs=inputs, segments=segments, padding=padding, first_gain=first_gain, first_shift=first_shift, second_gain=second_gain, second_shift=second_shift, joint_weight=joint_weight, joint_bias=joint_bias, dense_weight=dense_weight, dense_bias=dense_bias, expand_weight=expand_weight, expand_bias=expand_bias, reduce_weight=reduce_weight, reduce_bias=reduce_bias, cotangent=cotangent)


EPS = 1e-05
NEGATIVE = -1e+30
ROOT_HALF = 0.7071067811865476
ROOT_TWOPI = 2.5066282746310002

def normalize(matrix):
    centred = matrix - lax.optimization_barrier(jnp.mean(matrix, axis=1, keepdims=True))
    scale_inv = lax.rsqrt(lax.optimization_barrier(jnp.mean(centred * centred, axis=1, keepdims=True)) + EPS)
    return (centred * scale_inv, scale_inv)

def layout(labels):
    indices = jnp.arange(labels.shape[0])
    matching = labels[:, None] == labels[None, :]
    earlier = indices[None, :] < indices[:, None]
    positions = lax.optimization_barrier(jnp.sum((matching & earlier).astype(jnp.int32), axis=1)).astype(jnp.float32)
    allowed = matching & (indices[None, :] <= indices[:, None])
    return (positions, allowed)

def rotary_tables(positions):
    half_width = ROT // 2
    frequency = jnp.exp(jnp.arange(half_width, dtype=jnp.float32) * (-2.0 * math.log(10000.0) / ROT))
    angles = positions[:, None] * frequency[None, :]
    return (jnp.cos(angles)[:, None, :], jnp.sin(angles)[:, None, :])

def rotate(tensor, cosine_table, sine_table):
    half_width = ROT // 2
    leading = tensor[..., :half_width]
    trailing = tensor[..., half_width:ROT]
    remain = tensor[..., ROT:]
    return jnp.concatenate([leading * cosine_table - trailing * sine_table, trailing * cosine_table + leading * sine_table, remain], axis=-1)

def unrotate(tensor, cosine_table, sine_table):
    half_width = ROT // 2
    leading = tensor[..., :half_width]
    trailing = tensor[..., half_width:ROT]
    remain = tensor[..., ROT:]
    return jnp.concatenate([leading * cosine_table + trailing * sine_table, trailing * cosine_table - leading * sine_table, remain], axis=-1)

def gelu_value(values):
    return 0.5 * values * (1.0 + lax.erf(values * ROOT_HALF))

def gelu_slope(values):
    return 0.5 * (1.0 + lax.erf(values * ROOT_HALF)) + values * jnp.exp(-0.5 * values * values) / ROOT_TWOPI

def reference(inputs, segments, padding, first_gain, first_shift, second_gain, second_shift, joint_weight, joint_bias, dense_weight, dense_bias, expand_weight, expand_bias, reduce_weight, reduce_bias, cotangent):
    block_count = TOKENS // ROWS
    head_cols = D // N_MP
    unit_cols = FF // N_MP
    joint_cols = 3 * D // N_MP
    query_scale = HD ** (-0.5)
    gain_one = first_gain.astype(jnp.float32)
    gain_two = second_gain.astype(jnp.float32)

    def one_block(totals, pieces):
        rows_raw, labels, marks, grad_out = pieces
        rows_in = rows_raw.astype(jnp.float32)
        normed, scale_inv = normalize(rows_in)
        hidden_one = (normed * gain_one + first_shift.astype(jnp.float32)).astype(jnp.bfloat16)
        hidden_two = (normed * gain_two + second_shift.astype(jnp.float32)).astype(jnp.bfloat16)
        positions, allowed = layout(labels)
        cosine_table, sine_table = rotary_tables(positions)
        joint = (jnp.dot(hidden_one, joint_weight, preferred_element_type=jnp.float32) + joint_bias.astype(jnp.float32)).reshape(ROWS, H, 3, HD)
        queries = (rotate(joint[:, :, 0], cosine_table, sine_table) * query_scale).astype(jnp.bfloat16)
        key_rows = rotate(joint[:, :, 1], cosine_table, sine_table).astype(jnp.bfloat16)
        value_rows = joint[:, :, 2].astype(jnp.bfloat16)
        scores = jnp.einsum('qhd,khd->hqk', queries.astype(jnp.float32), key_rows.astype(jnp.float32))
        scores = jnp.where(allowed[None], scores, NEGATIVE)
        row_peak = lax.optimization_barrier(jnp.max(scores, axis=2, keepdims=True))
        logsum = row_peak + jnp.log(lax.optimization_barrier(jnp.sum(jnp.exp(scores - row_peak), axis=2, keepdims=True)))
        chances = jnp.exp(scores - logsum)
        weights = chances.astype(jnp.bfloat16)
        mixture = jnp.einsum('hqk,khd->qhd', weights.astype(jnp.float32), value_rows.astype(jnp.float32)).astype(jnp.bfloat16)
        mixture_flat = mixture.reshape(ROWS, D)
        before = jnp.dot(hidden_two, expand_weight, preferred_element_type=jnp.float32) + expand_bias.astype(jnp.float32)
        activated = gelu_value(before).astype(jnp.bfloat16)
        branches = jnp.zeros((ROWS, D), jnp.float32)
        for group_index in range(N_MP):
            head_slice = slice(group_index * head_cols, (group_index + 1) * head_cols)
            unit_slice = slice(group_index * unit_cols, (group_index + 1) * unit_cols)
            group_term = jnp.dot(mixture_flat[:, head_slice], dense_weight[head_slice], preferred_element_type=jnp.float32) + jnp.dot(activated[:, unit_slice], reduce_weight[unit_slice], preferred_element_type=jnp.float32)
            branches = branches + lax.optimization_barrier(group_term.astype(jnp.bfloat16)).astype(jnp.float32)
        result = (rows_in + branches + dense_bias.astype(jnp.float32) + reduce_bias.astype(jnp.float32)).astype(jnp.bfloat16)
        seed_grad = grad_out.astype(jnp.float32) * marks.astype(jnp.float32)[:, None]
        seed_low = seed_grad.astype(jnp.bfloat16)
        bias_grad = lax.optimization_barrier(jnp.sum(seed_grad, axis=0))
        dense_back = jnp.dot(mixture_flat.T, seed_low, preferred_element_type=jnp.float32)
        reduce_back = jnp.dot(activated.T, seed_low, preferred_element_type=jnp.float32)
        grad_mixture = jnp.dot(seed_low, dense_weight.T, preferred_element_type=jnp.float32).astype(jnp.bfloat16).reshape(ROWS, H, HD)
        before_grad = jnp.dot(seed_low, reduce_weight.T, preferred_element_type=jnp.float32) * gelu_slope(before)
        before_low = before_grad.astype(jnp.bfloat16)
        expand_back = jnp.dot(hidden_two.T, before_low, preferred_element_type=jnp.float32)
        expand_bias_back = lax.optimization_barrier(jnp.sum(before_grad, axis=0))
        value_grad = jnp.einsum('hqk,qhd->khd', weights.astype(jnp.float32), grad_mixture.astype(jnp.float32))
        weight_grad = jnp.einsum('qhd,khd->hqk', grad_mixture.astype(jnp.float32), value_rows.astype(jnp.float32))
        row_dot = lax.optimization_barrier(jnp.sum(grad_mixture.astype(jnp.float32) * mixture.astype(jnp.float32), axis=2)).T
        score_grad = (chances * (weight_grad - row_dot[:, :, None])).astype(jnp.bfloat16)
        query_grad = jnp.einsum('hqk,khd->qhd', score_grad.astype(jnp.float32), key_rows.astype(jnp.float32))
        key_grad = jnp.einsum('hqk,qhd->khd', score_grad.astype(jnp.float32), queries.astype(jnp.float32))
        joint_grad = jnp.stack([unrotate(query_grad * query_scale, cosine_table, sine_table), unrotate(key_grad, cosine_table, sine_table), value_grad], axis=2).reshape(ROWS, 3 * D)
        joint_low = joint_grad.astype(jnp.bfloat16)
        joint_back = jnp.dot(hidden_one.T, joint_low, preferred_element_type=jnp.float32)
        joint_bias_back = lax.optimization_barrier(jnp.sum(joint_grad, axis=0))
        grad_one = jnp.zeros((ROWS, D), jnp.float32)
        grad_two = jnp.zeros((ROWS, D), jnp.float32)
        for group_index in range(N_MP):
            joint_slice = slice(group_index * joint_cols, (group_index + 1) * joint_cols)
            unit_slice = slice(group_index * unit_cols, (group_index + 1) * unit_cols)
            term_one = jnp.dot(joint_low[:, joint_slice], joint_weight[:, joint_slice].T, preferred_element_type=jnp.float32)
            term_two = jnp.dot(before_low[:, unit_slice], expand_weight[:, unit_slice].T, preferred_element_type=jnp.float32)
            grad_one = grad_one + lax.optimization_barrier(term_one.astype(jnp.bfloat16)).astype(jnp.float32)
            grad_two = grad_two + lax.optimization_barrier(term_two.astype(jnp.bfloat16)).astype(jnp.float32)
        grad_normed = grad_one * gain_one + grad_two * gain_two
        inputs_back = (seed_grad + scale_inv * (grad_normed - lax.optimization_barrier(jnp.mean(grad_normed, axis=1, keepdims=True)) - normed * lax.optimization_barrier(jnp.mean(grad_normed * normed, axis=1, keepdims=True)))).astype(jnp.bfloat16)
        terms = (lax.optimization_barrier(jnp.sum(grad_one * normed, axis=0)), lax.optimization_barrier(jnp.sum(grad_one, axis=0)), lax.optimization_barrier(jnp.sum(grad_two * normed, axis=0)), lax.optimization_barrier(jnp.sum(grad_two, axis=0)), joint_back, joint_bias_back, dense_back, bias_grad, expand_back, expand_bias_back, reduce_back, bias_grad)
        totals = tuple((older + newer for older, newer in zip(totals, terms)))
        return (totals, (result, inputs_back))
    initial = (jnp.zeros((D,), jnp.float32), jnp.zeros((D,), jnp.float32), jnp.zeros((D,), jnp.float32), jnp.zeros((D,), jnp.float32), jnp.zeros((D, 3 * D), jnp.float32), jnp.zeros((3 * D,), jnp.float32), jnp.zeros((D, D), jnp.float32), jnp.zeros((D,), jnp.float32), jnp.zeros((D, FF), jnp.float32), jnp.zeros((FF,), jnp.float32), jnp.zeros((FF, D), jnp.float32), jnp.zeros((D,), jnp.float32))
    pieces = (inputs.reshape(block_count, ROWS, D), segments.reshape(block_count, ROWS), padding.reshape(block_count, ROWS), cotangent.reshape(block_count, ROWS, D))
    totals, (result, inputs_back) = lax.scan(one_block, initial, pieces)
    return (result.reshape(TOKENS, D), inputs_back.reshape(TOKENS, D), totals[0], totals[1], totals[2], totals[3], totals[4], totals[5], totals[6], totals[7], totals[8], totals[9], totals[10], totals[11])
```

```python
import math

import jax
import jax.numpy as jnp
from jax import lax
from jax.experimental import pallas as pl
from jax.experimental.pallas import tpu as pltpu
from jax.sharding import PartitionSpec as P

HD = 256
ROT = 64
BLOCK = 512
LANES = 128
PIECES = 8

EPS = 1e-05
NEGATIVE = -1e30
ROOT_HALF = 0.7071067811865476
ROOT_TWOPI = 2.5066282746310002
F32 = jnp.float32
BF16 = jnp.bfloat16


def nt(a, b):
    return lax.dot_general(a, b, (((1,), (1,)), ((), ())), preferred_element_type=F32)


def tn(a, b):
    return lax.dot_general(a, b, (((0,), (0,)), ((), ())), preferred_element_type=F32)


def nn(a, b):
    return lax.dot_general(a, b, (((1,), (0,)), ((), ())), preferred_element_type=F32)


def call(kernel, out_shape, flops, nbytes, extra=0, **more):
    return pl.pallas_call(
        kernel,
        out_shape=out_shape,
        compiler_params=pltpu.CompilerParams(vmem_limit_bytes=56 << 20),
        cost_estimate=pl.CostEstimate(
            flops=flops, bytes_accessed=nbytes, transcendentals=extra
        ),
        **more,
    )


def shape(*dims, dtype=BF16):
    return jax.ShapeDtypeStruct(dims, dtype)


def whole(*dims):
    return pl.BlockSpec(dims, lambda *_: (0,) * len(dims))


def folded(values):
    return jnp.sum(values.reshape(-1, 8, values.shape[1]), axis=0)


def accumulate(ref, at, values, first):
    @pl.when(first)
    def _():
        ref[:, at] = values

    @pl.when(jnp.logical_not(first))
    def _():
        ref[:, at] += values


def rows_kernel(
    where_ref, in_ref, cot_ref, pad_ref, vec_ref, one_ref, two_ref, norm_ref, seed_ref, sum_ref
):
    x = in_ref[...].astype(F32)
    mean = jnp.mean(x, axis=1, keepdims=True)
    centred = x - mean
    inv = lax.rsqrt(jnp.mean(centred * centred, axis=1, keepdims=True) + EPS)
    marks = pad_ref[...].astype(F32)
    width = x.shape[1] // PIECES
    first = pl.program_id(0) == 0
    for r in range(PIECES):
        source = pl.ds(pl.multiple_of(where_ref[r] * width, width), width)
        at = slice(r * width, (r + 1) * width)
        normed = (in_ref[:, source].astype(F32) - mean) * inv
        norm_ref[:, at] = normed.astype(BF16)
        one_ref[:, at] = (normed * vec_ref[0:1, at] + vec_ref[1:2, at]).astype(BF16)
        two_ref[:, at] = (normed * vec_ref[2:3, at] + vec_ref[3:4, at]).astype(BF16)
        seed = cot_ref[:, source].astype(F32) * marks
        seed_ref[:, at] = seed.astype(BF16)
        accumulate(sum_ref, at, folded(seed), first)


def rows_pass(where, inputs, cotangent, marks, vectors):
    total, features = inputs.shape
    tile = total // 8
    wide = pl.BlockSpec((tile, features), lambda i, w: (i, 0))
    return call(
        rows_kernel,
        [shape(total, features)] * 4 + [shape(8, features, dtype=F32)],
        40 * total * features,
        12 * total * features,
        grid_spec=pltpu.PrefetchScalarGridSpec(
            num_scalar_prefetch=1,
            grid=(8,),
            in_specs=[
                wide,
                wide,
                pl.BlockSpec((tile, 1), lambda i, w: (i, 0)),
                whole(vectors.shape[0], features),
            ],
            out_specs=[wide] * 4 + [whole(8, features)],
        ),
    )(where, inputs, cotangent, marks, vectors)


def joint_kernel(*refs):
    lhs, pieces, bias, out = refs[0], refs[1 : 1 + PIECES], refs[-2], refs[-1]
    weight = jnp.concatenate([p[...] for p in pieces], axis=0)
    out[...] = nn(lhs[...], weight) + bias[...]


def project(hidden, pieces, bias):
    total, features = hidden.shape
    depth, width = pieces[0].shape
    tile = 512
    return call(
        joint_kernel,
        shape(total, width, dtype=F32),
        2 * total * features * width,
        2 * features * (total + width) + 4 * total * width,
        grid=(width // tile,),
        in_specs=[whole(total, features)]
        + [pl.BlockSpec((depth, tile), lambda n: (0, n))] * PIECES
        + [pl.BlockSpec((1, tile), lambda n: (0, n))],
        out_specs=pl.BlockSpec((total, tile), lambda n: (0, n)),
    )(hidden, *pieces, bias)


def expand_kernel(*refs):
    lhs, pieces, bias, act, slope = refs[0], refs[1 : 1 + PIECES], refs[-3], refs[-2], refs[-1]
    weight = jnp.concatenate([p[...] for p in pieces], axis=0)
    u = nn(lhs[...], weight) + bias[...]
    phi = 0.5 * (1.0 + lax.erf(u * ROOT_HALF))
    act[...] = (u * phi).astype(BF16)
    slope[...] = (phi + u * jnp.exp(-0.5 * u * u) * (1.0 / ROOT_TWOPI)).astype(BF16)


def expand(hidden, pieces, bias):
    total, features = hidden.shape
    depth, width = pieces[0].shape
    tile = 256
    return call(
        expand_kernel,
        [shape(total, width)] * 2,
        2 * total * features * width,
        2 * features * (total + width) + 4 * total * width,
        2 * total * width,
        grid=(width // tile,),
        in_specs=[whole(total, features)]
        + [pl.BlockSpec((depth, tile), lambda n: (0, n))] * PIECES
        + [pl.BlockSpec((1, tile), lambda n: (0, n))],
        out_specs=[pl.BlockSpec((total, tile), lambda n: (0, n))] * 2,
    )(hidden, *pieces, bias)


def mixture_kernel(*refs):
    lhs, pieces, out = refs[0], refs[1 : 1 + PIECES], refs[-1]
    weight = jnp.concatenate([p[...] for p in pieces], axis=1)
    out[...] = nt(lhs[...], weight).astype(BF16)


def mixture_back(seed, pieces):
    total, features = seed.shape
    width, depth = pieces[0].shape
    tile = 256
    return call(
        mixture_kernel,
        shape(total, width),
        2 * total * features * width,
        2 * features * (total + width) + 2 * total * width,
        grid=(width // tile,),
        in_specs=[whole(total, features)]
        + [pl.BlockSpec((tile, depth), lambda n: (n, 0))] * PIECES,
        out_specs=pl.BlockSpec((total, tile), lambda n: (0, n)),
    )(seed, *pieces)


def before_kernel(*refs):
    lhs, pieces, slope, low, sums = refs[0], refs[1 : 1 + PIECES], refs[-3], refs[-2], refs[-1]
    weight = jnp.concatenate([p[...] for p in pieces], axis=1)
    grad = nt(lhs[...], weight) * slope[...].astype(F32)
    low[...] = grad.astype(BF16)
    sums[...] = folded(grad)


def before_back(seed, pieces, slope):
    total, features = seed.shape
    width, depth = pieces[0].shape
    tile = 512
    return call(
        before_kernel,
        [shape(total, width), shape(8, width, dtype=F32)],
        2 * total * features * width,
        2 * features * (total + width) + 4 * total * width,
        grid=(width // tile,),
        in_specs=[whole(total, features)]
        + [pl.BlockSpec((tile, depth), lambda n: (n, 0))] * PIECES
        + [pl.BlockSpec((total, tile), lambda n: (0, n))],
        out_specs=[
            pl.BlockSpec((total, tile), lambda n: (0, n)),
            pl.BlockSpec((8, tile), lambda n: (0, n)),
        ],
    )(seed, *pieces, slope)


def loads(pieces, scratch, sems):
    copies = []
    for r, p in enumerate(pieces):
        axis = 0 if scratch.shape[1] == 2 * p.shape[0] else 1
        side = pl.ds((r % 2) * p.shape[axis], p.shape[axis])
        slot = scratch.at[r // 2, side] if axis == 0 else scratch.at[r // 2, :, side]
        copies.append(pltpu.make_async_copy(p, slot, sems.at[r // 2]))
    return copies


def arrived(groups, at):
    @pl.when(at == 0)
    def _():
        for copies in zip(*(loads(*group) for group in groups)):
            for copy in copies:
                copy.start()

    for pieces, scratch, sems in groups:
        slot = scratch.at[at]
        pltpu.make_async_copy(slot, slot, sems.at[at]).wait()


def held(pieces, axis):
    rows, columns = pieces[0].shape
    slot = (2 * rows, columns) if axis == 0 else (rows, 2 * columns)
    return [
        pltpu.VMEM((PIECES // 2,) + slot, BF16),
        pltpu.SemaphoreType.DMA((PIECES // 2,)),
    ]


def branch_kernel(*refs):
    mix, act = refs[0], refs[1]
    dense, reduce = refs[2 : 2 + PIECES], refs[2 + PIECES : 2 + 2 * PIECES]
    out, dense_vm, dense_sem, reduce_vm, reduce_sem = refs[-5:]
    r = pl.program_id(0)
    arrived(((dense, dense_vm, dense_sem), (reduce, reduce_vm, reduce_sem)), r)
    out[...] = (nn(mix[...], dense_vm[r]) + nn(act[...], reduce_vm[r])).astype(BF16)


def branch_of(mixture, activated, dense, reduce):
    total = mixture.shape[0]
    width = dense[0].shape[1]
    depth = mixture.shape[1] + activated.shape[1]
    return call(
        branch_kernel,
        shape(total, PIECES * width),
        2 * total * depth * PIECES * width,
        2 * depth * (total + PIECES * width) + 2 * total * PIECES * width,
        grid=(PIECES // 2,),
        in_specs=[whole(*mixture.shape), whole(*activated.shape)]
        + [pl.BlockSpec(memory_space=pl.ANY)] * (2 * PIECES),
        out_specs=pl.BlockSpec((total, 2 * width), lambda r: (0, r)),
        scratch_shapes=held(dense, 1) + held(reduce, 1),
    )(mixture, activated, *dense, *reduce)


def gx_kernel(*refs):
    low_one, low_two, norm, vec = refs[:4]
    joint, wide = refs[4 : 4 + PIECES], refs[4 + PIECES : 4 + 2 * PIECES]
    out, gains, joint_vm, joint_sem, wide_vm, wide_sem = refs[-6:]
    r = pl.program_id(0)
    arrived(((joint, joint_vm, joint_sem), (wide, wide_vm, wide_sem)), r)
    one = nt(low_one[...], joint_vm[r])
    two = nt(low_two[...], wide_vm[r])
    out[...] = (one * vec[0:1, :] + two * vec[2:3, :]).astype(BF16)
    normed = norm[...].astype(F32)
    gains[0:8, :] = folded(one * normed)
    gains[8:16, :] = folded(one)
    gains[16:24, :] = folded(two * normed)
    gains[24:32, :] = folded(two)


def gx_of(joint_low, before_low, normed, vectors, joint, wide):
    total, features = normed.shape
    depth = joint_low.shape[1] + before_low.shape[1]
    each = 2 * features // PIECES
    return call(
        gx_kernel,
        [shape(total, features), shape(32, features, dtype=F32)],
        2 * total * depth * features,
        2 * depth * (total + features) + 4 * total * features,
        grid=(PIECES // 2,),
        in_specs=[
            whole(*joint_low.shape),
            whole(*before_low.shape),
            pl.BlockSpec((total, each), lambda r: (0, r)),
            pl.BlockSpec((vectors.shape[0], each), lambda r: (0, r)),
        ]
        + [pl.BlockSpec(memory_space=pl.ANY)] * (2 * PIECES),
        out_specs=[
            pl.BlockSpec((total, each), lambda r: (0, r)),
            pl.BlockSpec((32, each), lambda r: (0, r)),
        ],
        scratch_shapes=held(joint, 0) + held(wide, 0),
    )(joint_low, before_low, normed, vectors, *joint, *wide)


def gradient_kernel(where_ref, *refs):
    sides = len(refs) // 2
    lhs, rhs, out = refs[:sides], refs[sides : 2 * sides], refs[-1]
    start = 0
    for left, right in zip(lhs, rhs):
        stop = start + right.shape[1]
        out[:, start:stop] = tn(left[...], right[...]).astype(BF16)
        start = stop


def gradient(where, lhs, rhs):
    total, features = lhs[0].shape
    width = sum(a.shape[1] for a in rhs)
    each = features // PIECES
    return call(
        gradient_kernel,
        shape(features, width),
        2 * total * features * width,
        2 * len(lhs) * total * features + 2 * total * width + 2 * features * width,
        grid_spec=pltpu.PrefetchScalarGridSpec(
            num_scalar_prefetch=1,
            grid=(PIECES,),
            in_specs=[pl.BlockSpec((total, each), lambda r, w: (0, r))] * len(lhs)
            + [whole(*a.shape) for a in rhs],
            out_specs=pl.BlockSpec((each, width), lambda r, w: (w[r], 0)),
        ),
    )(where, *lhs, *rhs)


def rotary_tables(segments):
    rows = segments.reshape(-1, BLOCK)
    indices = jnp.arange(BLOCK)
    matching = rows[:, :, None] == rows[:, None, :]
    earlier = indices[None, :] < indices[:, None]
    positions = jnp.sum((matching & earlier[None]).astype(jnp.int32), axis=2)
    positions = positions.astype(F32).reshape(-1)
    half = ROT // 2
    frequency = jnp.exp(jnp.arange(half, dtype=F32) * (-2.0 * math.log(10000.0) / ROT))
    angles = positions[:, None] * frequency[None, :]
    cosine, sine = jnp.cos(angles), jnp.sin(angles)
    pad = jnp.ones((angles.shape[0], LANES - ROT), F32)
    return (
        jnp.concatenate([cosine, cosine, pad], axis=1),
        jnp.concatenate([-sine, sine, 0.0 * pad], axis=1),
    )


def swap_halves(first):
    lane = lax.broadcasted_iota(jnp.int32, first.shape, 1)
    return jnp.where(
        lane < ROT // 2,
        pltpu.roll(first, LANES - ROT // 2, 1),
        pltpu.roll(first, ROT // 2, 1),
    )


def attend_kernel(
    joint_ref, grad_ref, cos_ref, sin_ref, col_ref, row_ref, mix_ref, low_ref, bias_ref
):
    cosine, sine = cos_ref[...], sin_ref[...]

    def rotate(t):
        first = t[:, :LANES]
        return jnp.concatenate(
            [first * cosine + swap_halves(first) * sine, t[:, LANES:]], axis=1
        )

    def unrotate(t):
        first = t[:, :LANES]
        return jnp.concatenate(
            [first * cosine - swap_halves(first) * sine, t[:, LANES:]], axis=1
        )

    scale = HD ** (-0.5)
    queries = (rotate(joint_ref[:, :HD]) * scale).astype(BF16)
    keys = rotate(joint_ref[:, HD : 2 * HD]).astype(BF16)
    values = joint_ref[:, 2 * HD :].astype(BF16)
    grad = grad_ref[...]
    scores = nt(queries, keys)
    size = scores.shape
    allowed = (col_ref[...] == row_ref[0]) & (
        lax.broadcasted_iota(jnp.int32, size, 1) <= lax.broadcasted_iota(jnp.int32, size, 0)
    )
    scores = jnp.where(allowed, scores, NEGATIVE)
    peak = jnp.max(scores, axis=1, keepdims=True)
    chances = jnp.exp(scores - peak)
    chances = chances * (1.0 / jnp.sum(chances, axis=1, keepdims=True))
    weights = chances.astype(BF16)
    mixture = nn(weights, values).astype(BF16)
    mix_ref[...] = mixture
    value_grad = tn(weights, grad)
    weight_grad = nt(grad, values)
    delta = jnp.sum(grad.astype(F32) * mixture.astype(F32), axis=1, keepdims=True)
    score_grad = (chances * (weight_grad - delta)).astype(BF16)
    query_grad = unrotate(nn(score_grad, keys)) * scale
    key_grad = unrotate(tn(score_grad, queries))
    first = pl.program_id(1) == 0
    for at, piece in enumerate((query_grad, key_grad, value_grad)):
        at = slice(at * HD, (at + 1) * HD)
        low_ref[:, at] = piece.astype(BF16)
        accumulate(bias_ref, at, folded(piece), first)


def attend(joint, grad_mixture, cosine, sine, column, segments):
    total, width = joint.shape
    heads, blocks = width // (3 * HD), total // BLOCK
    table = pl.BlockSpec((BLOCK, LANES), lambda h, b: (b, 0))
    wide = pl.BlockSpec((BLOCK, 3 * HD), lambda h, b: (b, h))
    narrow = pl.BlockSpec((BLOCK, HD), lambda h, b: (b, h))
    return call(
        attend_kernel,
        [shape(total, heads * HD), shape(total, width), shape(8, width, dtype=F32)],
        14 * total * BLOCK * heads * HD,
        total * width * 8,
        total * BLOCK * heads,
        grid=(heads, blocks),
        in_specs=[
            wide,
            narrow,
            table,
            table,
            pl.BlockSpec((BLOCK, 1), lambda h, b: (b, 0)),
            pl.BlockSpec((1, 1, BLOCK), lambda h, b: (b, 0, 0)),
        ],
        out_specs=[narrow, wide, pl.BlockSpec((8, 3 * HD), lambda h, b: (0, h))],
    )(
        joint,
        grad_mixture,
        cosine,
        sine,
        column,
        segments.reshape(blocks, 1, BLOCK),
    )


def result_kernel(where_ref, in_ref, got_ref, vec_ref, out_ref):
    width = in_ref.shape[1] // PIECES
    for r in range(PIECES):
        target = pl.ds(pl.multiple_of(where_ref[r] * width, width), width)
        at = slice(r * width, (r + 1) * width)
        total = got_ref[:, at].astype(F32) + in_ref[:, target].astype(F32) + vec_ref[4:5, at]
        out_ref[:, target] = total.astype(BF16)


def back_kernel(
    where_ref, in_ref, cot_ref, pad_ref, own_ref, below_ref, above_ref, out_ref, sum_ref
):
    x = in_ref[...].astype(F32)
    mean = jnp.mean(x, axis=1, keepdims=True)
    centred = x - mean
    inv = lax.rsqrt(jnp.mean(centred * centred, axis=1, keepdims=True) + EPS)
    features = x.shape[1]
    width = features // PIECES
    plain = jnp.zeros_like(mean)
    crossed = jnp.zeros_like(mean)
    for r in range(PIECES):
        target = pl.ds(pl.multiple_of(where_ref[r] * width, width), width)
        at = slice(r * width, (r + 1) * width)
        total = (
            own_ref[:, at].astype(F32)
            + below_ref[:, at].astype(F32)
            + above_ref[:, at].astype(F32)
        )
        sum_ref[:, at] = total
        plain += jnp.sum(total, axis=1, keepdims=True)
        normed = (in_ref[:, target].astype(F32) - mean) * inv
        crossed += jnp.sum(total * normed, axis=1, keepdims=True)
    plain = plain * (1.0 / features)
    crossed = crossed * (1.0 / features)
    marks = pad_ref[...].astype(F32)
    for r in range(PIECES):
        target = pl.ds(pl.multiple_of(where_ref[r] * width, width), width)
        at = slice(r * width, (r + 1) * width)
        normed = (in_ref[:, target].astype(F32) - mean) * inv
        seed = cot_ref[:, target].astype(F32) * marks
        out_ref[:, target] = (
            seed + inv * (sum_ref[:, at] - plain - normed * crossed)
        ).astype(BF16)


def finish(kernel, where, half, own_rows, got, tail, scratch=()):
    features = own_rows[0].shape[1]
    tile = got[0][1]
    row = (lambda at: at[PIECES]) if half is None else (lambda at: at[PIECES] * 2 + half)
    own = lambda w: pl.BlockSpec((tile, w), lambda i, at: (row(at), 0))
    here = lambda a: pl.BlockSpec(
        (tile, features), lambda i, at: (half if a.shape[0] > tile else 0, 0)
    )
    return call(
        kernel,
        shape(tile, features),
        20 * tile * features,
        12 * tile * features,
        grid_spec=pltpu.PrefetchScalarGridSpec(
            num_scalar_prefetch=1,
            grid=(1,),
            in_specs=[own(a.shape[1]) for a in own_rows]
            + [here(a) for a, _ in got]
            + [whole(*a.shape) for a in tail],
            out_specs=pl.BlockSpec((tile, features), lambda i, at: (0, 0)),
            scratch_shapes=[pltpu.VMEM((tile, features), F32)] * len(scratch),
        ),
    )(where, *own_rows, *(a for a, _ in got), *tail)


def swapped(a, bit):
    return lax.ppermute(a, "dp", [(i, i ^ bit) for i in range(PIECES)])


def crossed_over(from_x, from_y):
    core = lax.axis_index("dp") & 1
    pairs = [(i, i ^ (4 if i & 1 else 2)) for i in range(PIECES)]
    return lax.ppermute(jnp.where(core == 1, from_x, from_y), "dp", pairs)


def gather_pieces(items, after):
    gathered, arrived = {}, {}
    for name, own in items:
        if name in after:
            own, _ = lax.optimization_barrier((own, arrived[after[name]]))
        from_x = swapped(own, 2)
        from_y = swapped(own, 4)
        arrived[name] = (from_x, from_y)
        diagonal = crossed_over(from_x, from_y)
        near = (own, from_x, from_y, diagonal)
        far = [swapped(a, 1) for a in near]
        gathered[name] = [b for pair in zip(near, far) for b in pair]
    return gathered


def scattered_small(values):
    for bit in (4, 2, 1):
        values = values[:bit] + swapped(values[bit:], bit)
    return values[0]


def neighbours(t, spreading):
    n = lax.axis_size("mp")
    up = [(z, z + 1) for z in (range(t - 1, n - 1) if spreading else range(min(t, n - 1)))]
    return up, [(n - 1 - a, n - 1 - b) for a, b in up]


def summed_rows(part):
    n, me = lax.axis_size("mp"), lax.axis_index("mp")
    share = part.shape[0] // n
    tile = share // 2
    block = lambda j, half: lax.dynamic_slice_in_dim(
        part, jnp.clip(j, 0, n - 1) * share + half * tile, tile, 0
    )
    going = [(block(n - 1 + me, half), block(1 + me - n, half)) for half in (0, 1)]
    going = lax.optimization_barrier(going)
    got = [None, None]
    for t in range(1, n):
        up, down = neighbours(t, False)
        for half in (0, 1):
            if t > 1:
                pair = block(n - t + me, half), block(t + me - n, half)
                going[half] = lax.optimization_barrier(
                    tuple(mine + theirs for mine, theirs in zip(pair, got[half]))
                )
            got[half] = (
                lax.ppermute(going[half][0], "mp", up), lax.ppermute(going[half][1], "mp", down)
            )
    return got


def spread_rows(parts, room, late=None):
    n, me = lax.axis_size("mp"), lax.axis_index("mp")
    tile = parts[0].shape[0]
    rights, lefts = [parts], [parts]
    for t in range(1, n):
        up, down = neighbours(t, True)
        right, left = [], []
        if t == n - 1 and late is not None:
            rights[-1], lefts[-1], late = lax.optimization_barrier((rights[-1], lefts[-1], late))
        for i in range(len(parts)):
            right.append(lax.ppermute(rights[-1][i], "mp", up))
            left.append(lax.ppermute(lefts[-1][i], "mp", down))
        rights.append(right)
        lefts.append(left)
    for t in range(n):
        for i in range(len(parts)):
            rows = parts[i] if t == 0 else lefts[t][i] + rights[n - t][i]
            at = (lax.rem(me + t, n) * len(parts) + i) * tile
            room = lax.dynamic_update_slice_in_dim(room, rows, at, 0)
    return room, late


def summed_over_mp(values):
    n = lax.axis_size("mp")
    if n & (n - 1):
        return lax.psum(values, "mp")
    bit = 1
    while bit < n:
        pairs = [(z, z ^ bit) for z in range(n)]
        values = values + lax.ppermute(values, "mp", pairs)
        bit *= 2
    return values


def step(
    inputs,
    segments,
    padding,
    first_gain,
    first_shift,
    second_gain,
    second_shift,
    joint_weight,
    joint_bias,
    dense_weight,
    dense_bias,
    expand_weight,
    expand_bias,
    reduce_weight,
    reduce_bias,
    cotangent,
):
    total, features = inputs.shape
    n_dp = lax.axis_size("dp")
    dp_at, mp_at = lax.axis_index("dp"), lax.axis_index("mp")
    order = jnp.arange(PIECES, dtype=jnp.int32)
    small = (
        joint_bias, expand_bias, first_gain, first_shift, second_gain, second_shift,
        dense_bias, reduce_bias,
    )
    longest = max(a.shape[0] for a in small)
    line = lax.broadcasted_iota(jnp.int32, (len(small), longest), 0)
    packed = jnp.zeros((len(small), longest), BF16)
    for i, a in enumerate(small):
        packed = jnp.where(line == i, jnp.pad(a, (0, longest - a.shape[0]))[None], packed)
    if n_dp == PIECES:
        order = dp_at ^ order
        packed = packed[None]
        packed = jnp.concatenate([packed, swapped(packed, 1)], axis=0)
        packed = jnp.concatenate([packed] + [swapped(packed, bit) for bit in (2, 4, 6)], axis=0)
        blocks = gather_pieces(
            (
                ("D", dense_weight),
                ("E", expand_weight),
                ("J", joint_weight),
                ("R", reduce_weight),
            ),
            {"R": "J"},
        )
        dense, joint_w, wide, reduce = (blocks[k] for k in "DJER")
        padding, segments, packed = lax.optimization_barrier((padding, segments, packed))
        by_device = jnp.take(packed, order, axis=0)
    else:
        packed = by_device = lax.all_gather(packed, "dp")
        rows = lambda a: jnp.split(lax.all_gather(a, "dp", axis=0, tiled=True), PIECES, 0)
        columns = lambda a: jnp.split(lax.all_gather(a, "dp", axis=1, tiled=True), PIECES, 1)
        dense, joint_w = columns(dense_weight), rows(joint_weight)
        wide, reduce = rows(expand_weight), columns(reduce_weight)
    where = jnp.concatenate([order, mp_at[None].astype(jnp.int32)])
    taken = lambda a, i: a[:, i, : small[i].shape[0]].reshape(1, -1).astype(F32)
    bias_j, bias_e = taken(by_device, 0), taken(by_device, 1)
    vectors = jnp.concatenate(
        [taken(packed, i) for i in range(2, 6)]
        + [taken(packed, 6) + taken(packed, 7), jnp.zeros((3, features), F32)]
    )

    marks = padding[:, None]
    hidden_one, hidden_two, normed, seed, bias_back = rows_pass(
        where, inputs, cotangent, marks, vectors
    )
    cosine, sine = rotary_tables(segments)
    column = segments.reshape(total, 1)
    cosine, sine, column, hidden_two = lax.optimization_barrier(
        (cosine, sine, column, hidden_two)
    )

    grad_mixture = mixture_back(seed, dense)
    joint = project(hidden_one, joint_w, bias_j)
    mixture, joint_low, joint_bias_back = attend(joint, grad_mixture, cosine, sine, column, segments)
    activated, slope = expand(hidden_two, wide, bias_e)
    branch = branch_of(mixture, activated, dense, reduce)
    before_low, expand_bias_back = before_back(seed, reduce, slope)
    gx, gains = gx_of(joint_low, before_low, normed, vectors, joint_w, wide)

    tile = total // lax.axis_size("mp") // 2
    branches = lax.psum_scatter(branch, "mp", scatter_dimension=0, tiled=True)
    result = finish(
        result_kernel, where, None, (inputs,), ((branches, 2 * tile),),
        (vectors,),
    )
    result, _ = spread_rows([result], branch)
    grads = gradient(
        where, (hidden_one, seed, hidden_two, seed),
        (joint_low, mixture, before_low, activated),
    )
    grads, _ = lax.optimization_barrier((grads, branches))
    grads = lax.psum_scatter(grads, "dp", scatter_dimension=0, tiled=True)
    cuts = [0]
    for a in (joint_low, mixture, before_low, activated):
        cuts.append(cuts[-1] + a.shape[1])
    piece = lambda i: grads[:, cuts[i] : cuts[i + 1]].astype(F32)
    weights = (piece(0), piece(1).T, piece(2), piece(3).T)

    back = [
        finish(back_kernel, where, half, (inputs, cotangent, marks, gx),
              tuple((a, tile) for a in got), (), (0,))
        for half, got in enumerate(summed_rows(gx))
    ]
    back, weights = spread_rows(back, gx, weights)

    gains = jnp.sum(gains.reshape(4, 8, features), axis=1)
    gains = summed_over_mp(gains)
    straight = jnp.concatenate([gains, jnp.sum(bias_back, axis=0)[None]])
    by_row = [
        jnp.sum(joint_bias_back, axis=0).reshape(n_dp, -1),
        jnp.sum(expand_bias_back, axis=0).reshape(n_dp, -1),
    ]
    if n_dp == PIECES:
        by_row = [jnp.take(a, order, axis=0) for a in by_row]
    sums = jnp.concatenate(
        by_row + [straight[i].reshape(n_dp, -1) for i in range(5)], axis=1
    )
    if n_dp == PIECES:
        sums = scattered_small(sums)
    else:
        sums = lax.psum_scatter(sums, "dp", scatter_dimension=0, tiled=True).reshape(-1)
    widths = [joint_bias.shape[0], expand_bias.shape[0]] + [features // n_dp] * 5
    cuts = [sum(widths[:i]) for i in range(len(widths) + 1)]
    parts = [sums[a:b] for a, b in zip(cuts, cuts[1:])]
    return (
        result, back, parts[2], parts[3], parts[4], parts[5],
        weights[0], parts[0], weights[1], parts[6],
        weights[2], parts[1], weights[3], parts[6],
    )


def solution(mesh):
    placed = (
        P("dp", None), P("dp"), P("dp"), P("dp"), P("dp"), P("dp"), P("dp"),
        P("dp", "mp"), P(("mp", "dp")), P("mp", "dp"), P("dp"),
        P("dp", "mp"), P(("mp", "dp")), P("mp", "dp"), P("dp"), P("dp", None),
    )
    return jax.shard_map(
        step,
        mesh=mesh,
        in_specs=placed,
        out_specs=(
            P("dp", None), P("dp", None), P("dp"), P("dp"), P("dp"), P("dp"),
            P("dp", "mp"), P(("mp", "dp")), P("mp", "dp"), P("dp"),
            P("dp", "mp"), P(("mp", "dp")), P("mp", "dp"), P("dp"),
        ),
        check_vma=False,
    )
```

```python
import math

import jax
import jax.numpy as jnp
from jax import lax
from jax.experimental import pallas as pl
from jax.experimental.pallas import tpu as pltpu
from jax.sharding import PartitionSpec as P

HD = 256
ROT = 64
BLOCK = 512
LANES = 128
PIECES = 8

EPS = 1e-05
NEGATIVE = -1e30
ROOT_HALF = 0.7071067811865476
ROOT_TWOPI = 2.5066282746310002
F32 = jnp.float32
BF16 = jnp.bfloat16


def nt(a, b):
    return lax.dot_general(a, b, (((1,), (1,)), ((), ())), preferred_element_type=F32)


def tn(a, b):
    return lax.dot_general(a, b, (((0,), (0,)), ((), ())), preferred_element_type=F32)


def nn(a, b):
    return lax.dot_general(a, b, (((1,), (0,)), ((), ())), preferred_element_type=F32)


def call(kernel, out_shape, flops, nbytes, extra=0, **more):
    return pl.pallas_call(
        kernel,
        out_shape=out_shape,
        compiler_params=pltpu.CompilerParams(vmem_limit_bytes=56 << 20),
        cost_estimate=pl.CostEstimate(
            flops=flops, bytes_accessed=nbytes, transcendentals=extra
        ),
        **more,
    )


def shape(*dims, dtype=BF16):
    return jax.ShapeDtypeStruct(dims, dtype)


def whole(*dims):
    return pl.BlockSpec(dims, lambda *_: (0,) * len(dims))


def folded(values):
    return jnp.sum(values.reshape(-1, 8, values.shape[1]), axis=0)


def accumulate(ref, at, values, first):
    @pl.when(first)
    def _():
        ref[:, at] = values

    @pl.when(jnp.logical_not(first))
    def _():
        ref[:, at] += values


def rows_kernel(
    where_ref, in_ref, cot_ref, pad_ref, vec_ref, one_ref, two_ref, norm_ref, seed_ref, sum_ref
):
    x = in_ref[...].astype(F32)
    mean = jnp.mean(x, axis=1, keepdims=True)
    centred = x - mean
    inv = lax.rsqrt(jnp.mean(centred * centred, axis=1, keepdims=True) + EPS)
    marks = pad_ref[...].astype(F32)
    width = x.shape[1] // PIECES
    first = pl.program_id(0) == 0
    for r in range(PIECES):
        source = pl.ds(pl.multiple_of(where_ref[r] * width, width), width)
        at = slice(r * width, (r + 1) * width)
        normed = (in_ref[:, source].astype(F32) - mean) * inv
        norm_ref[:, at] = normed.astype(BF16)
        one_ref[:, at] = (normed * vec_ref[0:1, at] + vec_ref[1:2, at]).astype(BF16)
        two_ref[:, at] = (normed * vec_ref[2:3, at] + vec_ref[3:4, at]).astype(BF16)
        seed = cot_ref[:, source].astype(F32) * marks
        seed_ref[:, at] = seed.astype(BF16)
        accumulate(sum_ref, at, folded(seed), first)


def rows_pass(where, inputs, cotangent, marks, vectors):
    total, features = inputs.shape
    tile = total // 8
    wide = pl.BlockSpec((tile, features), lambda i, w: (i, 0))
    return call(
        rows_kernel,
        [shape(total, features)] * 4 + [shape(8, features, dtype=F32)],
        40 * total * features,
        12 * total * features,
        grid_spec=pltpu.PrefetchScalarGridSpec(
            num_scalar_prefetch=1,
            grid=(8,),
            in_specs=[
                wide,
                wide,
                pl.BlockSpec((tile, 1), lambda i, w: (i, 0)),
                whole(vectors.shape[0], features),
            ],
            out_specs=[wide] * 4 + [whole(8, features)],
        ),
    )(where, inputs, cotangent, marks, vectors)


def joint_kernel(*refs):
    lhs, pieces, bias, out = refs[0], refs[1 : 1 + PIECES], refs[-2], refs[-1]
    weight = jnp.concatenate([p[...] for p in pieces], axis=0)
    out[...] = nn(lhs[...], weight) + bias[...]


def project(hidden, pieces, bias):
    total, features = hidden.shape
    depth, width = pieces[0].shape
    tile = 512
    return call(
        joint_kernel,
        shape(total, width, dtype=F32),
        2 * total * features * width,
        2 * features * (total + width) + 4 * total * width,
        grid=(width // tile,),
        in_specs=[whole(total, features)]
        + [pl.BlockSpec((depth, tile), lambda n: (0, n))] * PIECES
        + [pl.BlockSpec((1, tile), lambda n: (0, n))],
        out_specs=pl.BlockSpec((total, tile), lambda n: (0, n)),
    )(hidden, *pieces, bias)


def expand_kernel(*refs):
    lhs, pieces, bias, act, slope = refs[0], refs[1 : 1 + PIECES], refs[-3], refs[-2], refs[-1]
    weight = jnp.concatenate([p[...] for p in pieces], axis=0)
    u = nn(lhs[...], weight) + bias[...]
    phi = 0.5 * (1.0 + lax.erf(u * ROOT_HALF))
    act[...] = (u * phi).astype(BF16)
    slope[...] = (phi + u * jnp.exp(-0.5 * u * u) * (1.0 / ROOT_TWOPI)).astype(BF16)


def expand(hidden, pieces, bias):
    total, features = hidden.shape
    depth, width = pieces[0].shape
    tile = 256
    return call(
        expand_kernel,
        [shape(total, width)] * 2,
        2 * total * features * width,
        2 * features * (total + width) + 4 * total * width,
        2 * total * width,
        grid=(width // tile,),
        in_specs=[whole(total, features)]
        + [pl.BlockSpec((depth, tile), lambda n: (0, n))] * PIECES
        + [pl.BlockSpec((1, tile), lambda n: (0, n))],
        out_specs=[pl.BlockSpec((total, tile), lambda n: (0, n))] * 2,
    )(hidden, *pieces, bias)


def mixture_kernel(*refs):
    lhs, pieces, out = refs[0], refs[1 : 1 + PIECES], refs[-1]
    weight = jnp.concatenate([p[...] for p in pieces], axis=1)
    out[...] = nt(lhs[...], weight).astype(BF16)


def mixture_back(seed, pieces):
    total, features = seed.shape
    width, depth = pieces[0].shape
    tile = 256
    return call(
        mixture_kernel,
        shape(total, width),
        2 * total * features * width,
        2 * features * (total + width) + 2 * total * width,
        grid=(width // tile,),
        in_specs=[whole(total, features)]
        + [pl.BlockSpec((tile, depth), lambda n: (n, 0))] * PIECES,
        out_specs=pl.BlockSpec((total, tile), lambda n: (0, n)),
    )(seed, *pieces)


def before_kernel(*refs):
    lhs, pieces, slope, low, sums = refs[0], refs[1 : 1 + PIECES], refs[-3], refs[-2], refs[-1]
    weight = jnp.concatenate([p[...] for p in pieces], axis=1)
    grad = nt(lhs[...], weight) * slope[...].astype(F32)
    low[...] = grad.astype(BF16)
    sums[...] = folded(grad)


def before_back(seed, pieces, slope):
    total, features = seed.shape
    width, depth = pieces[0].shape
    tile = 512
    return call(
        before_kernel,
        [shape(total, width), shape(8, width, dtype=F32)],
        2 * total * features * width,
        2 * features * (total + width) + 4 * total * width,
        grid=(width // tile,),
        in_specs=[whole(total, features)]
        + [pl.BlockSpec((tile, depth), lambda n: (n, 0))] * PIECES
        + [pl.BlockSpec((total, tile), lambda n: (0, n))],
        out_specs=[
            pl.BlockSpec((total, tile), lambda n: (0, n)),
            pl.BlockSpec((8, tile), lambda n: (0, n)),
        ],
    )(seed, *pieces, slope)


def loads(pieces, scratch, sems):
    copies = []
    for r, p in enumerate(pieces):
        axis = 0 if scratch.shape[1] == 2 * p.shape[0] else 1
        side = pl.ds((r % 2) * p.shape[axis], p.shape[axis])
        slot = scratch.at[r // 2, side] if axis == 0 else scratch.at[r // 2, :, side]
        copies.append(pltpu.make_async_copy(p, slot, sems.at[r // 2]))
    return copies


def arrived(groups, at):
    @pl.when(at == 0)
    def _():
        for copies in zip(*(loads(*group) for group in groups)):
            for copy in copies:
                copy.start()

    for pieces, scratch, sems in groups:
        slot = scratch.at[at]
        pltpu.make_async_copy(slot, slot, sems.at[at]).wait()


def held(pieces, axis):
    rows, columns = pieces[0].shape
    slot = (2 * rows, columns) if axis == 0 else (rows, 2 * columns)
    return [
        pltpu.VMEM((PIECES // 2,) + slot, BF16),
        pltpu.SemaphoreType.DMA((PIECES // 2,)),
    ]


def branch_kernel(*refs):
    mix, act = refs[0], refs[1]
    dense, reduce = refs[2 : 2 + PIECES], refs[2 + PIECES : 2 + 2 * PIECES]
    out, dense_vm, dense_sem, reduce_vm, reduce_sem = refs[-5:]
    r = pl.program_id(0)
    arrived(((dense, dense_vm, dense_sem), (reduce, reduce_vm, reduce_sem)), r)
    out[...] = (nn(mix[...], dense_vm[r]) + nn(act[...], reduce_vm[r])).astype(BF16)


def branch_of(mixture, activated, dense, reduce):
    total = mixture.shape[0]
    width = dense[0].shape[1]
    depth = mixture.shape[1] + activated.shape[1]
    return call(
        branch_kernel,
        shape(total, PIECES * width),
        2 * total * depth * PIECES * width,
        2 * depth * (total + PIECES * width) + 2 * total * PIECES * width,
        grid=(PIECES // 2,),
        in_specs=[whole(*mixture.shape), whole(*activated.shape)]
        + [pl.BlockSpec(memory_space=pl.ANY)] * (2 * PIECES),
        out_specs=pl.BlockSpec((total, 2 * width), lambda r: (0, r)),
        scratch_shapes=held(dense, 1) + held(reduce, 1),
    )(mixture, activated, *dense, *reduce)


def gx_kernel(*refs):
    low_one, low_two, norm, vec = refs[:4]
    joint, wide = refs[4 : 4 + PIECES], refs[4 + PIECES : 4 + 2 * PIECES]
    out, gains, joint_vm, joint_sem, wide_vm, wide_sem = refs[-6:]
    r = pl.program_id(0)
    arrived(((joint, joint_vm, joint_sem), (wide, wide_vm, wide_sem)), r)
    one = nt(low_one[...], joint_vm[r])
    two = nt(low_two[...], wide_vm[r])
    out[...] = (one * vec[0:1, :] + two * vec[2:3, :]).astype(BF16)
    normed = norm[...].astype(F32)
    gains[0:8, :] = folded(one * normed)
    gains[8:16, :] = folded(one)
    gains[16:24, :] = folded(two * normed)
    gains[24:32, :] = folded(two)


def gx_of(joint_low, before_low, normed, vectors, joint, wide):
    total, features = normed.shape
    depth = joint_low.shape[1] + before_low.shape[1]
    each = 2 * features // PIECES
    return call(
        gx_kernel,
        [shape(total, features), shape(32, features, dtype=F32)],
        2 * total * depth * features,
        2 * depth * (total + features) + 4 * total * features,
        grid=(PIECES // 2,),
        in_specs=[
            whole(*joint_low.shape),
            whole(*before_low.shape),
            pl.BlockSpec((total, each), lambda r: (0, r)),
            pl.BlockSpec((vectors.shape[0], each), lambda r: (0, r)),
        ]
        + [pl.BlockSpec(memory_space=pl.ANY)] * (2 * PIECES),
        out_specs=[
            pl.BlockSpec((total, each), lambda r: (0, r)),
            pl.BlockSpec((32, each), lambda r: (0, r)),
        ],
        scratch_shapes=held(joint, 0) + held(wide, 0),
    )(joint_low, before_low, normed, vectors, *joint, *wide)


def gradient_kernel(where_ref, *refs):
    sides = len(refs) // 2
    lhs, rhs, out = refs[:sides], refs[sides : 2 * sides], refs[-1]
    start = 0
    for left, right in zip(lhs, rhs):
        stop = start + right.shape[1]
        out[:, start:stop] = tn(left[...], right[...]).astype(BF16)
        start = stop


def gradient(where, lhs, rhs):
    total, features = lhs[0].shape
    width = sum(a.shape[1] for a in rhs)
    each = features // PIECES
    return call(
        gradient_kernel,
        shape(features, width),
        2 * total * features * width,
        2 * len(lhs) * total * features + 2 * total * width + 2 * features * width,
        grid_spec=pltpu.PrefetchScalarGridSpec(
            num_scalar_prefetch=1,
            grid=(PIECES,),
            in_specs=[pl.BlockSpec((total, each), lambda r, w: (0, r))] * len(lhs)
            + [whole(*a.shape) for a in rhs],
            out_specs=pl.BlockSpec((each, width), lambda r, w: (w[r], 0)),
        ),
    )(where, *lhs, *rhs)


def unpack_kernel(in_ref, *outs):
    start = 0
    for i, out in enumerate(outs):
        width = out.shape[i % 2 == 0]
        for at in range(0, width, 256):
            block = in_ref[:, start + at : start + at + 256].astype(F32)
            if i % 2 == 0:
                out[:, at : at + 256] = block
            else:
                out[at : at + 256, :] = block.T
        start += width


def unpack(grads, widths):
    rows = grads.shape[0]
    return call(
        unpack_kernel,
        [
            shape(*((rows, w) if i % 2 == 0 else (w, rows)), dtype=F32)
            for i, w in enumerate(widths)
        ],
        rows * sum(widths),
        6 * rows * sum(widths),
    )(grads)


def rotary_tables(segments):
    rows = segments.reshape(-1, BLOCK)
    indices = jnp.arange(BLOCK)
    matching = rows[:, :, None] == rows[:, None, :]
    earlier = indices[None, :] < indices[:, None]
    positions = jnp.sum((matching & earlier[None]).astype(jnp.int32), axis=2)
    positions = positions.astype(F32).reshape(-1)
    half = ROT // 2
    frequency = jnp.exp(jnp.arange(half, dtype=F32) * (-2.0 * math.log(10000.0) / ROT))
    angles = positions[:, None] * frequency[None, :]
    cosine, sine = jnp.cos(angles), jnp.sin(angles)
    pad = jnp.ones((angles.shape[0], LANES - ROT), F32)
    return (
        jnp.concatenate([cosine, cosine, pad], axis=1),
        jnp.concatenate([-sine, sine, 0.0 * pad], axis=1),
    )


def swap_halves(first):
    lane = lax.broadcasted_iota(jnp.int32, first.shape, 1)
    return jnp.where(
        lane < ROT // 2,
        pltpu.roll(first, LANES - ROT // 2, 1),
        pltpu.roll(first, ROT // 2, 1),
    )


def attend_kernel(
    joint_ref, grad_ref, cos_ref, sin_ref, col_ref, row_ref, mix_ref, low_ref, bias_ref
):
    cosine, sine = cos_ref[...], sin_ref[...]

    def rotate(t):
        first = t[:, :LANES]
        return jnp.concatenate(
            [first * cosine + swap_halves(first) * sine, t[:, LANES:]], axis=1
        )

    def unrotate(t):
        first = t[:, :LANES]
        return jnp.concatenate(
            [first * cosine - swap_halves(first) * sine, t[:, LANES:]], axis=1
        )

    scale = HD ** (-0.5)
    queries = (rotate(joint_ref[:, :HD]) * scale).astype(BF16)
    keys = rotate(joint_ref[:, HD : 2 * HD]).astype(BF16)
    values = joint_ref[:, 2 * HD :].astype(BF16)
    grad = grad_ref[...]
    scores = nt(queries, keys)
    size = scores.shape
    allowed = (col_ref[...] == row_ref[0]) & (
        lax.broadcasted_iota(jnp.int32, size, 1) <= lax.broadcasted_iota(jnp.int32, size, 0)
    )
    scores = jnp.where(allowed, scores, NEGATIVE)
    peak = jnp.max(scores, axis=1, keepdims=True)
    chances = jnp.exp(scores - peak)
    chances = chances * (1.0 / jnp.sum(chances, axis=1, keepdims=True))
    weights = chances.astype(BF16)
    mixture = nn(weights, values).astype(BF16)
    mix_ref[...] = mixture
    value_grad = tn(weights, grad)
    weight_grad = nt(grad, values)
    delta = jnp.sum(grad.astype(F32) * mixture.astype(F32), axis=1, keepdims=True)
    score_grad = (chances * (weight_grad - delta)).astype(BF16)
    query_grad = unrotate(nn(score_grad, keys)) * scale
    key_grad = unrotate(tn(score_grad, queries))
    first = pl.program_id(1) == 0
    for at, piece in enumerate((query_grad, key_grad, value_grad)):
        at = slice(at * HD, (at + 1) * HD)
        low_ref[:, at] = piece.astype(BF16)
        accumulate(bias_ref, at, folded(piece), first)


def attend(joint, grad_mixture, cosine, sine, column, segments):
    total, width = joint.shape
    heads, blocks = width // (3 * HD), total // BLOCK
    table = pl.BlockSpec((BLOCK, LANES), lambda h, b: (b, 0))
    wide = pl.BlockSpec((BLOCK, 3 * HD), lambda h, b: (b, h))
    narrow = pl.BlockSpec((BLOCK, HD), lambda h, b: (b, h))
    return call(
        attend_kernel,
        [shape(total, heads * HD), shape(total, width), shape(8, width, dtype=F32)],
        14 * total * BLOCK * heads * HD,
        total * width * 8,
        total * BLOCK * heads,
        grid=(heads, blocks),
        in_specs=[
            wide,
            narrow,
            table,
            table,
            pl.BlockSpec((BLOCK, 1), lambda h, b: (b, 0)),
            pl.BlockSpec((1, 1, BLOCK), lambda h, b: (b, 0, 0)),
        ],
        out_specs=[narrow, wide, pl.BlockSpec((8, 3 * HD), lambda h, b: (0, h))],
    )(
        joint,
        grad_mixture,
        cosine,
        sine,
        column,
        segments.reshape(blocks, 1, BLOCK),
    )


def result_kernel(where_ref, in_ref, got_ref, vec_ref, out_ref):
    width = in_ref.shape[1] // PIECES
    for r in range(PIECES):
        target = pl.ds(pl.multiple_of(where_ref[r] * width, width), width)
        at = slice(r * width, (r + 1) * width)
        total = got_ref[:, at].astype(F32) + in_ref[:, target].astype(F32) + vec_ref[4:5, at]
        out_ref[:, target] = total.astype(BF16)


def back_kernel(
    where_ref, in_ref, cot_ref, pad_ref, own_ref, below_ref, above_ref, out_ref, sum_ref
):
    x = in_ref[...].astype(F32)
    mean = jnp.mean(x, axis=1, keepdims=True)
    centred = x - mean
    inv = lax.rsqrt(jnp.mean(centred * centred, axis=1, keepdims=True) + EPS)
    features = x.shape[1]
    width = features // PIECES
    plain = jnp.zeros_like(mean)
    crossed = jnp.zeros_like(mean)
    for r in range(PIECES):
        target = pl.ds(pl.multiple_of(where_ref[r] * width, width), width)
        at = slice(r * width, (r + 1) * width)
        total = (
            own_ref[:, at].astype(F32)
            + below_ref[:, at].astype(F32)
            + above_ref[:, at].astype(F32)
        )
        sum_ref[:, at] = total
        plain += jnp.sum(total, axis=1, keepdims=True)
        normed = (in_ref[:, target].astype(F32) - mean) * inv
        crossed += jnp.sum(total * normed, axis=1, keepdims=True)
    plain = plain * (1.0 / features)
    crossed = crossed * (1.0 / features)
    marks = pad_ref[...].astype(F32)
    for r in range(PIECES):
        target = pl.ds(pl.multiple_of(where_ref[r] * width, width), width)
        at = slice(r * width, (r + 1) * width)
        normed = (in_ref[:, target].astype(F32) - mean) * inv
        seed = cot_ref[:, target].astype(F32) * marks
        out_ref[:, target] = (
            seed + inv * (sum_ref[:, at] - plain - normed * crossed)
        ).astype(BF16)


def finish(kernel, where, half, own_rows, got, tail, scratch=()):
    features = own_rows[0].shape[1]
    tile = got[0][1]
    row = (lambda at: at[PIECES]) if half is None else (lambda at: at[PIECES] * 2 + half)
    own = lambda w: pl.BlockSpec((tile, w), lambda i, at: (row(at), 0))
    here = lambda a: pl.BlockSpec(
        (tile, features), lambda i, at: (half if a.shape[0] > tile else 0, 0)
    )
    return call(
        kernel,
        shape(tile, features),
        20 * tile * features,
        12 * tile * features,
        grid_spec=pltpu.PrefetchScalarGridSpec(
            num_scalar_prefetch=1,
            grid=(1,),
            in_specs=[own(a.shape[1]) for a in own_rows]
            + [here(a) for a, _ in got]
            + [whole(*a.shape) for a in tail],
            out_specs=pl.BlockSpec((tile, features), lambda i, at: (0, 0)),
            scratch_shapes=[pltpu.VMEM((tile, features), F32)] * len(scratch),
        ),
    )(where, *own_rows, *(a for a, _ in got), *tail)


def swapped(a, bit):
    return lax.ppermute(a, "dp", [(i, i ^ bit) for i in range(PIECES)])


def crossed_over(from_x, from_y):
    core = lax.axis_index("dp") & 1
    pairs = [(i, i ^ (4 if i & 1 else 2)) for i in range(PIECES)]
    return lax.ppermute(jnp.where(core == 1, from_x, from_y), "dp", pairs)


def gather_pieces(items, after):
    gathered, arrived = {}, {}
    for name, own in items:
        if name in after:
            own, _ = lax.optimization_barrier((own, arrived[after[name]]))
        from_x = swapped(own, 2)
        from_y = swapped(own, 4)
        arrived[name] = (from_x, from_y)
        diagonal = crossed_over(from_x, from_y)
        near = (own, from_x, from_y, diagonal)
        far = [swapped(a, 1) for a in near]
        gathered[name] = [b for pair in zip(near, far) for b in pair]
    return gathered


def scattered_small(values):
    for bit in (4, 2, 1):
        values = values[:bit] + swapped(values[bit:], bit)
    return values[0]


def neighbours(t, spreading):
    n = lax.axis_size("mp")
    up = [(z, z + 1) for z in (range(t - 1, n - 1) if spreading else range(min(t, n - 1)))]
    return up, [(n - 1 - a, n - 1 - b) for a, b in up]


def leaving_kernel(at_ref, *refs):
    refs, outs = refs[:-2], refs[-2:]
    for i, out in enumerate(outs):
        rows = refs[i][...].astype(F32)
        if len(refs) > 2:
            rows = rows + refs[2 + i][...].astype(F32)
        out[...] = rows.astype(BF16)


def leaving(at, part, tile, got):
    features = part.shape[1]
    step = tile // 2
    own = lambda which: pl.BlockSpec((step, features), lambda i, at: (2 * at[which] + i, 0))
    here = pl.BlockSpec((step, features), lambda i, at: (i, 0))
    return call(
        leaving_kernel,
        [shape(tile, features)] * 2,
        2 * tile * features,
        (4 + 2 * len(got)) * tile * features * 2,
        grid_spec=pltpu.PrefetchScalarGridSpec(
            num_scalar_prefetch=1,
            grid=(2,),
            in_specs=[own(0), own(1)] + [here] * len(got),
            out_specs=[here] * 2,
        ),
    )(at, part, part, *got)


def summed_rows(part):
    n, me = lax.axis_size("mp"), lax.axis_index("mp")
    share = part.shape[0] // n
    tile = share // 2
    got = [(), ()]
    for t in range(1, n):
        up, down = neighbours(t, False)
        for half in (0, 1):
            blocks = jnp.stack([jnp.clip(n - t + me, 0, n - 1), jnp.clip(t + me - n, 0, n - 1)])
            going = leaving(2 * blocks.astype(jnp.int32) + half, part, tile, got[half])
            got[half] = (lax.ppermute(going[0], "mp", up), lax.ppermute(going[1], "mp", down))
    return got


def spread_rows(parts, room, late=None):
    n, me = lax.axis_size("mp"), lax.axis_index("mp")
    tile = parts[0].shape[0]
    rights, lefts = [parts], [parts]
    for t in range(1, n):
        up, down = neighbours(t, True)
        right, left = [], []
        for i in range(len(parts)):
            right.append(lax.ppermute(rights[-1][i], "mp", up))
            left.append(lax.ppermute(lefts[-1][i], "mp", down))
        rights.append(right)
        lefts.append(left)
    if late is not None:
        room, late = lax.optimization_barrier((room, late))
    for t in range(n):
        for i in range(len(parts)):
            rows = parts[i] if t == 0 else lefts[t][i] + rights[n - t][i]
            at = (lax.rem(me + t, n) * len(parts) + i) * tile
            room = lax.dynamic_update_slice_in_dim(room, rows, at, 0)
    return room, late


def summed_over_mp(values):
    n = lax.axis_size("mp")
    if n & (n - 1):
        return lax.psum(values, "mp")
    bit = 1
    while bit < n:
        pairs = [(z, z ^ bit) for z in range(n)]
        values = values + lax.ppermute(values, "mp", pairs)
        bit *= 2
    return values


def step(
    inputs,
    segments,
    padding,
    first_gain,
    first_shift,
    second_gain,
    second_shift,
    joint_weight,
    joint_bias,
    dense_weight,
    dense_bias,
    expand_weight,
    expand_bias,
    reduce_weight,
    reduce_bias,
    cotangent,
):
    total, features = inputs.shape
    n_dp = lax.axis_size("dp")
    dp_at, mp_at = lax.axis_index("dp"), lax.axis_index("mp")
    order = jnp.arange(PIECES, dtype=jnp.int32)
    small = (
        joint_bias, expand_bias, first_gain, first_shift, second_gain, second_shift,
        dense_bias, reduce_bias,
    )
    longest = max(a.shape[0] for a in small)
    line = lax.broadcasted_iota(jnp.int32, (len(small), longest), 0)
    packed = jnp.zeros((len(small), longest), BF16)
    for i, a in enumerate(small):
        packed = jnp.where(line == i, jnp.pad(a, (0, longest - a.shape[0]))[None], packed)
    if n_dp == PIECES:
        order = dp_at ^ order
        packed = packed[None]
        packed = jnp.concatenate([packed, swapped(packed, 1)], axis=0)
        packed = jnp.concatenate([packed] + [swapped(packed, bit) for bit in (2, 4, 6)], axis=0)
        blocks = gather_pieces(
            (
                ("D", dense_weight),
                ("E", expand_weight),
                ("J", joint_weight),
                ("R", reduce_weight),
            ),
            {"R": "J"},
        )
        dense, joint_w, wide, reduce = (blocks[k] for k in "DJER")
        padding, segments, packed = lax.optimization_barrier((padding, segments, packed))
        by_device = jnp.take(packed, order, axis=0)
    else:
        packed = by_device = lax.all_gather(packed, "dp")
        rows = lambda a: jnp.split(lax.all_gather(a, "dp", axis=0, tiled=True), PIECES, 0)
        columns = lambda a: jnp.split(lax.all_gather(a, "dp", axis=1, tiled=True), PIECES, 1)
        dense, joint_w = columns(dense_weight), rows(joint_weight)
        wide, reduce = rows(expand_weight), columns(reduce_weight)
    where = jnp.concatenate([order, mp_at[None].astype(jnp.int32)])
    taken = lambda a, i: a[:, i, : small[i].shape[0]].reshape(1, -1).astype(F32)
    bias_j, bias_e = taken(by_device, 0), taken(by_device, 1)
    vectors = jnp.concatenate(
        [taken(packed, i) for i in range(2, 6)]
        + [taken(packed, 6) + taken(packed, 7), jnp.zeros((3, features), F32)]
    )

    marks = padding[:, None]
    hidden_one, hidden_two, normed, seed, bias_back = rows_pass(
        where, inputs, cotangent, marks, vectors
    )
    cosine, sine = rotary_tables(segments)
    column = segments.reshape(total, 1)
    cosine, sine, column, seed = lax.optimization_barrier((cosine, sine, column, seed))

    grad_mixture = mixture_back(seed, dense)
    joint = project(hidden_one, joint_w, bias_j)
    mixture, joint_low, joint_bias_back = attend(joint, grad_mixture, cosine, sine, column, segments)
    activated, slope = expand(hidden_two, wide, bias_e)
    branch = branch_of(mixture, activated, dense, reduce)
    before_low, expand_bias_back = before_back(seed, reduce, slope)
    gx, gains = gx_of(joint_low, before_low, normed, vectors, joint_w, wide)

    tile = total // lax.axis_size("mp") // 2
    branches = lax.psum_scatter(branch, "mp", scatter_dimension=0, tiled=True)
    result = finish(
        result_kernel, where, None, (inputs,), ((branches, 2 * tile),),
        (vectors,),
    )
    result, _ = spread_rows([result], branch)
    grads = gradient(
        where, (hidden_one, seed, hidden_two, seed),
        (joint_low, mixture, before_low, activated),
    )
    grads, _ = lax.optimization_barrier((grads, branches))
    grads = lax.psum_scatter(grads, "dp", scatter_dimension=0, tiled=True)
    widths = [a.shape[1] for a in (joint_low, mixture, before_low, activated)]
    weights = unpack(grads, widths)

    back = [
        finish(back_kernel, where, half, (inputs, cotangent, marks, gx),
              tuple((a, tile) for a in got), (), (0,))
        for half, got in enumerate(summed_rows(gx))
    ]
    back, weights = spread_rows(back, normed, weights)

    gains = jnp.sum(gains.reshape(4, 8, features), axis=1)
    gains = summed_over_mp(gains)
    straight = jnp.concatenate([gains, jnp.sum(bias_back, axis=0)[None]])
    by_row = [
        jnp.sum(joint_bias_back, axis=0).reshape(n_dp, -1),
        jnp.sum(expand_bias_back, axis=0).reshape(n_dp, -1),
    ]
    if n_dp == PIECES:
        by_row = [jnp.take(a, order, axis=0) for a in by_row]
    sums = jnp.concatenate(
        by_row + [straight[i].reshape(n_dp, -1) for i in range(5)], axis=1
    )
    if n_dp == PIECES:
        sums = scattered_small(sums)
    else:
        sums = lax.psum_scatter(sums, "dp", scatter_dimension=0, tiled=True).reshape(-1)
    widths = [joint_bias.shape[0], expand_bias.shape[0]] + [features // n_dp] * 5
    cuts = [sum(widths[:i]) for i in range(len(widths) + 1)]
    parts = [sums[a:b] for a, b in zip(cuts, cuts[1:])]
    return (
        result, back, parts[2], parts[3], parts[4], parts[5],
        weights[0], parts[0], weights[1], parts[6],
        weights[2], parts[1], weights[3], parts[6],
    )


def solution(mesh):
    placed = (
        P("dp", None), P("dp"), P("dp"), P("dp"), P("dp"), P("dp"), P("dp"),
        P("dp", "mp"), P(("mp", "dp")), P("mp", "dp"), P("dp"),
        P("dp", "mp"), P(("mp", "dp")), P("mp", "dp"), P("dp"), P("dp", None),
    )
    return jax.shard_map(
        step,
        mesh=mesh,
        in_specs=placed,
        out_specs=(
            P("dp", None), P("dp", None), P("dp"), P("dp"), P("dp"), P("dp"),
            P("dp", "mp"), P(("mp", "dp")), P("mp", "dp"), P("dp"),
            P("dp", "mp"), P(("mp", "dp")), P("mp", "dp"), P("dp"),
        ),
        check_vma=False,
    )
```

```python
import math

import jax
import jax.numpy as jnp
from jax import lax
from jax.experimental import pallas as pl
from jax.experimental.pallas import tpu as pltpu
from jax.sharding import PartitionSpec as P

HD = 256
ROT = 64
BLOCK = 512
LANES = 128
PIECES = 8

EPS = 1e-05
NEGATIVE = -1e30
ROOT_HALF = 0.7071067811865476
ROOT_TWOPI = 2.5066282746310002
F32 = jnp.float32
BF16 = jnp.bfloat16


def nt(a, b):
    return lax.dot_general(a, b, (((1,), (1,)), ((), ())), preferred_element_type=F32)


def tn(a, b):
    return lax.dot_general(a, b, (((0,), (0,)), ((), ())), preferred_element_type=F32)


def nn(a, b):
    return lax.dot_general(a, b, (((1,), (0,)), ((), ())), preferred_element_type=F32)


def call(kernel, out_shape, flops, nbytes, extra=0, **more):
    return pl.pallas_call(
        kernel,
        out_shape=out_shape,
        compiler_params=pltpu.CompilerParams(vmem_limit_bytes=56 << 20),
        cost_estimate=pl.CostEstimate(
            flops=flops, bytes_accessed=nbytes, transcendentals=extra
        ),
        **more,
    )


def shape(*dims, dtype=BF16):
    return jax.ShapeDtypeStruct(dims, dtype)


def whole(*dims):
    return pl.BlockSpec(dims, lambda *_: (0,) * len(dims))


def folded(values):
    return jnp.sum(values.reshape(-1, 8, values.shape[1]), axis=0)


def accumulate(ref, at, values, first):
    @pl.when(first)
    def _():
        ref[:, at] = values

    @pl.when(jnp.logical_not(first))
    def _():
        ref[:, at] += values


def rows_kernel(
    where_ref, in_ref, cot_ref, pad_ref, vec_ref, one_ref, two_ref, norm_ref, seed_ref, sum_ref
):
    x = in_ref[...].astype(F32)
    mean = jnp.mean(x, axis=1, keepdims=True)
    centred = x - mean
    inv = lax.rsqrt(jnp.mean(centred * centred, axis=1, keepdims=True) + EPS)
    marks = pad_ref[...].astype(F32)
    width = x.shape[1] // PIECES
    first = pl.program_id(0) == 0
    for r in range(PIECES):
        source = pl.ds(pl.multiple_of(where_ref[r] * width, width), width)
        at = slice(r * width, (r + 1) * width)
        normed = (in_ref[:, source].astype(F32) - mean) * inv
        norm_ref[:, at] = normed.astype(BF16)
        one_ref[:, at] = (normed * vec_ref[0:1, at] + vec_ref[1:2, at]).astype(BF16)
        two_ref[:, at] = (normed * vec_ref[2:3, at] + vec_ref[3:4, at]).astype(BF16)
        seed = cot_ref[:, source].astype(F32) * marks
        seed_ref[:, at] = seed.astype(BF16)
        accumulate(sum_ref, at, folded(seed), first)


def rows_pass(where, inputs, cotangent, marks, vectors):
    total, features = inputs.shape
    tile = total // 8
    wide = pl.BlockSpec((tile, features), lambda i, w: (i, 0))
    return call(
        rows_kernel,
        [shape(total, features)] * 4 + [shape(8, features, dtype=F32)],
        40 * total * features,
        12 * total * features,
        grid_spec=pltpu.PrefetchScalarGridSpec(
            num_scalar_prefetch=1,
            grid=(8,),
            in_specs=[
                wide,
                wide,
                pl.BlockSpec((tile, 1), lambda i, w: (i, 0)),
                whole(vectors.shape[0], features),
            ],
            out_specs=[wide] * 4 + [whole(8, features)],
        ),
    )(where, inputs, cotangent, marks, vectors)


def joint_kernel(*refs):
    lhs, pieces, bias, out = refs[0], refs[1 : 1 + PIECES], refs[-2], refs[-1]
    weight = jnp.concatenate([p[...] for p in pieces], axis=0)
    out[...] = nn(lhs[...], weight) + bias[...]


def project(hidden, pieces, bias):
    total, features = hidden.shape
    depth, width = pieces[0].shape
    tile = 512
    return call(
        joint_kernel,
        shape(total, width, dtype=F32),
        2 * total * features * width,
        2 * features * (total + width) + 4 * total * width,
        grid=(width // tile,),
        in_specs=[whole(total, features)]
        + [pl.BlockSpec((depth, tile), lambda n: (0, n))] * PIECES
        + [pl.BlockSpec((1, tile), lambda n: (0, n))],
        out_specs=pl.BlockSpec((total, tile), lambda n: (0, n)),
    )(hidden, *pieces, bias)


def expand_kernel(*refs):
    lhs, pieces, bias, act, slope = refs[0], refs[1 : 1 + PIECES], refs[-3], refs[-2], refs[-1]
    weight = jnp.concatenate([p[...] for p in pieces], axis=0)
    u = nn(lhs[...], weight) + bias[...]
    phi = 0.5 * (1.0 + lax.erf(u * ROOT_HALF))
    act[...] = (u * phi).astype(BF16)
    slope[...] = (phi + u * jnp.exp(-0.5 * u * u) * (1.0 / ROOT_TWOPI)).astype(BF16)


def expand(hidden, pieces, bias):
    total, features = hidden.shape
    depth, width = pieces[0].shape
    tile = 256
    return call(
        expand_kernel,
        [shape(total, width)] * 2,
        2 * total * features * width,
        2 * features * (total + width) + 4 * total * width,
        2 * total * width,
        grid=(width // tile,),
        in_specs=[whole(total, features)]
        + [pl.BlockSpec((depth, tile), lambda n: (0, n))] * PIECES
        + [pl.BlockSpec((1, tile), lambda n: (0, n))],
        out_specs=[pl.BlockSpec((total, tile), lambda n: (0, n))] * 2,
    )(hidden, *pieces, bias)


def mixture_kernel(*refs):
    lhs, pieces, out = refs[0], refs[1 : 1 + PIECES], refs[-1]
    weight = jnp.concatenate([p[...] for p in pieces], axis=1)
    out[...] = nt(lhs[...], weight).astype(BF16)


def mixture_back(seed, pieces):
    total, features = seed.shape
    width, depth = pieces[0].shape
    tile = 256
    return call(
        mixture_kernel,
        shape(total, width),
        2 * total * features * width,
        2 * features * (total + width) + 2 * total * width,
        grid=(width // tile,),
        in_specs=[whole(total, features)]
        + [pl.BlockSpec((tile, depth), lambda n: (n, 0))] * PIECES,
        out_specs=pl.BlockSpec((total, tile), lambda n: (0, n)),
    )(seed, *pieces)


def before_kernel(*refs):
    lhs, pieces, slope, low, sums = refs[0], refs[1 : 1 + PIECES], refs[-3], refs[-2], refs[-1]
    weight = jnp.concatenate([p[...] for p in pieces], axis=1)
    grad = nt(lhs[...], weight) * slope[...].astype(F32)
    low[...] = grad.astype(BF16)
    sums[...] = folded(grad)


def before_back(seed, pieces, slope):
    total, features = seed.shape
    width, depth = pieces[0].shape
    tile = 512
    return call(
        before_kernel,
        [shape(total, width), shape(8, width, dtype=F32)],
        2 * total * features * width,
        2 * features * (total + width) + 4 * total * width,
        grid=(width // tile,),
        in_specs=[whole(total, features)]
        + [pl.BlockSpec((tile, depth), lambda n: (n, 0))] * PIECES
        + [pl.BlockSpec((total, tile), lambda n: (0, n))],
        out_specs=[
            pl.BlockSpec((total, tile), lambda n: (0, n)),
            pl.BlockSpec((8, tile), lambda n: (0, n)),
        ],
    )(seed, *pieces, slope)


def loads(pieces, scratch, sems):
    copies = []
    for r, p in enumerate(pieces):
        axis = 0 if scratch.shape[1] == 2 * p.shape[0] else 1
        side = pl.ds((r % 2) * p.shape[axis], p.shape[axis])
        slot = scratch.at[r // 2, side] if axis == 0 else scratch.at[r // 2, :, side]
        copies.append(pltpu.make_async_copy(p, slot, sems.at[r // 2]))
    return copies


def arrived(groups, at):
    @pl.when(at == 0)
    def _():
        for copies in zip(*(loads(*group) for group in groups)):
            for copy in copies:
                copy.start()

    for pieces, scratch, sems in groups:
        slot = scratch.at[at]
        pltpu.make_async_copy(slot, slot, sems.at[at]).wait()


def held(pieces, axis):
    rows, columns = pieces[0].shape
    slot = (2 * rows, columns) if axis == 0 else (rows, 2 * columns)
    return [
        pltpu.VMEM((PIECES // 2,) + slot, BF16),
        pltpu.SemaphoreType.DMA((PIECES // 2,)),
    ]


def branch_kernel(*refs):
    mix, act = refs[0], refs[1]
    dense, reduce = refs[2 : 2 + PIECES], refs[2 + PIECES : 2 + 2 * PIECES]
    out, dense_vm, dense_sem, reduce_vm, reduce_sem = refs[-5:]
    r = pl.program_id(0)
    arrived(((dense, dense_vm, dense_sem), (reduce, reduce_vm, reduce_sem)), r)
    out[...] = (nn(mix[...], dense_vm[r]) + nn(act[...], reduce_vm[r])).astype(BF16)


def branch_of(mixture, activated, dense, reduce):
    total = mixture.shape[0]
    width = dense[0].shape[1]
    depth = mixture.shape[1] + activated.shape[1]
    return call(
        branch_kernel,
        shape(total, PIECES * width),
        2 * total * depth * PIECES * width,
        2 * depth * (total + PIECES * width) + 2 * total * PIECES * width,
        grid=(PIECES // 2,),
        in_specs=[whole(*mixture.shape), whole(*activated.shape)]
        + [pl.BlockSpec(memory_space=pl.ANY)] * (2 * PIECES),
        out_specs=pl.BlockSpec((total, 2 * width), lambda r: (0, r)),
        scratch_shapes=held(dense, 1) + held(reduce, 1),
    )(mixture, activated, *dense, *reduce)


def gx_kernel(*refs):
    low_one, low_two, norm, vec = refs[:4]
    joint, wide = refs[4 : 4 + PIECES], refs[4 + PIECES : 4 + 2 * PIECES]
    out, gains, joint_vm, joint_sem, wide_vm, wide_sem = refs[-6:]
    r = pl.program_id(0)
    arrived(((joint, joint_vm, joint_sem), (wide, wide_vm, wide_sem)), r)
    one = nt(low_one[...], joint_vm[r])
    two = nt(low_two[...], wide_vm[r])
    out[...] = (one * vec[0:1, :] + two * vec[2:3, :]).astype(BF16)
    normed = norm[...].astype(F32)
    gains[0:8, :] = folded(one * normed)
    gains[8:16, :] = folded(one)
    gains[16:24, :] = folded(two * normed)
    gains[24:32, :] = folded(two)


def gx_of(joint_low, before_low, normed, vectors, joint, wide):
    total, features = normed.shape
    depth = joint_low.shape[1] + before_low.shape[1]
    each = 2 * features // PIECES
    return call(
        gx_kernel,
        [shape(total, features), shape(32, features, dtype=F32)],
        2 * total * depth * features,
        2 * depth * (total + features) + 4 * total * features,
        grid=(PIECES // 2,),
        in_specs=[
            whole(*joint_low.shape),
            whole(*before_low.shape),
            pl.BlockSpec((total, each), lambda r: (0, r)),
            pl.BlockSpec((vectors.shape[0], each), lambda r: (0, r)),
        ]
        + [pl.BlockSpec(memory_space=pl.ANY)] * (2 * PIECES),
        out_specs=[
            pl.BlockSpec((total, each), lambda r: (0, r)),
            pl.BlockSpec((32, each), lambda r: (0, r)),
        ],
        scratch_shapes=held(joint, 0) + held(wide, 0),
    )(joint_low, before_low, normed, vectors, *joint, *wide)


def gradient_kernel(where_ref, *refs):
    sides = len(refs) // 2
    lhs, rhs, out = refs[:sides], refs[sides : 2 * sides], refs[-1]
    start = 0
    for left, right in zip(lhs, rhs):
        stop = start + right.shape[1]
        out[:, start:stop] = tn(left[...], right[...]).astype(BF16)
        start = stop


def gradient(where, lhs, rhs):
    total, features = lhs[0].shape
    width = sum(a.shape[1] for a in rhs)
    each = features // PIECES
    return call(
        gradient_kernel,
        shape(features, width),
        2 * total * features * width,
        2 * len(lhs) * total * features + 2 * total * width + 2 * features * width,
        grid_spec=pltpu.PrefetchScalarGridSpec(
            num_scalar_prefetch=1,
            grid=(PIECES,),
            in_specs=[pl.BlockSpec((total, each), lambda r, w: (0, r))] * len(lhs)
            + [whole(*a.shape) for a in rhs],
            out_specs=pl.BlockSpec((each, width), lambda r, w: (w[r], 0)),
        ),
    )(where, *lhs, *rhs)


def unpack_kernel(in_ref, *outs):
    start = 0
    for i, out in enumerate(outs):
        width = out.shape[i % 2 == 0]
        for at in range(0, width, 256):
            block = in_ref[:, start + at : start + at + 256].astype(F32)
            if i % 2 == 0:
                out[:, at : at + 256] = block
            else:
                out[at : at + 256, :] = block.T
        start += width


def unpack(grads, widths):
    rows = grads.shape[0]
    return call(
        unpack_kernel,
        [
            shape(*((rows, w) if i % 2 == 0 else (w, rows)), dtype=F32)
            for i, w in enumerate(widths)
        ],
        rows * sum(widths),
        6 * rows * sum(widths),
    )(grads)


def rotary_tables(segments):
    rows = segments.reshape(-1, BLOCK)
    indices = jnp.arange(BLOCK)
    matching = rows[:, :, None] == rows[:, None, :]
    earlier = indices[None, :] < indices[:, None]
    positions = jnp.sum((matching & earlier[None]).astype(jnp.int32), axis=2)
    positions = positions.astype(F32).reshape(-1)
    half = ROT // 2
    frequency = jnp.exp(jnp.arange(half, dtype=F32) * (-2.0 * math.log(10000.0) / ROT))
    angles = positions[:, None] * frequency[None, :]
    cosine, sine = jnp.cos(angles), jnp.sin(angles)
    pad = jnp.ones((angles.shape[0], LANES - ROT), F32)
    return (
        jnp.concatenate([cosine, cosine, pad], axis=1),
        jnp.concatenate([-sine, sine, 0.0 * pad], axis=1),
    )


def swap_halves(first):
    lane = lax.broadcasted_iota(jnp.int32, first.shape, 1)
    return jnp.where(
        lane < ROT // 2,
        pltpu.roll(first, LANES - ROT // 2, 1),
        pltpu.roll(first, ROT // 2, 1),
    )


def attend_kernel(
    joint_ref, grad_ref, cos_ref, sin_ref, col_ref, row_ref, mix_ref, low_ref, bias_ref
):
    cosine, sine = cos_ref[...], sin_ref[...]

    def rotate(t):
        first = t[:, :LANES]
        return jnp.concatenate(
            [first * cosine + swap_halves(first) * sine, t[:, LANES:]], axis=1
        )

    def unrotate(t):
        first = t[:, :LANES]
        return jnp.concatenate(
            [first * cosine - swap_halves(first) * sine, t[:, LANES:]], axis=1
        )

    scale = HD ** (-0.5)
    queries = (rotate(joint_ref[:, :HD]) * scale).astype(BF16)
    keys = rotate(joint_ref[:, HD : 2 * HD]).astype(BF16)
    values = joint_ref[:, 2 * HD :].astype(BF16)
    grad = grad_ref[...]
    scores = nt(queries, keys)
    size = scores.shape
    allowed = (col_ref[...] == row_ref[0]) & (
        lax.broadcasted_iota(jnp.int32, size, 1) <= lax.broadcasted_iota(jnp.int32, size, 0)
    )
    scores = jnp.where(allowed, scores, NEGATIVE)
    peak = jnp.max(scores, axis=1, keepdims=True)
    chances = jnp.exp(scores - peak)
    chances = chances * (1.0 / jnp.sum(chances, axis=1, keepdims=True))
    weights = chances.astype(BF16)
    mixture = nn(weights, values).astype(BF16)
    mix_ref[...] = mixture
    value_grad = tn(weights, grad)
    weight_grad = nt(grad, values)
    delta = jnp.sum(grad.astype(F32) * mixture.astype(F32), axis=1, keepdims=True)
    score_grad = (chances * (weight_grad - delta)).astype(BF16)
    query_grad = unrotate(nn(score_grad, keys)) * scale
    key_grad = unrotate(tn(score_grad, queries))
    first = pl.program_id(1) == 0
    for at, piece in enumerate((query_grad, key_grad, value_grad)):
        at = slice(at * HD, (at + 1) * HD)
        low_ref[:, at] = piece.astype(BF16)
        accumulate(bias_ref, at, folded(piece), first)


def attend(joint, grad_mixture, cosine, sine, column, segments):
    total, width = joint.shape
    heads, blocks = width // (3 * HD), total // BLOCK
    table = pl.BlockSpec((BLOCK, LANES), lambda h, b: (b, 0))
    wide = pl.BlockSpec((BLOCK, 3 * HD), lambda h, b: (b, h))
    narrow = pl.BlockSpec((BLOCK, HD), lambda h, b: (b, h))
    return call(
        attend_kernel,
        [shape(total, heads * HD), shape(total, width), shape(8, width, dtype=F32)],
        14 * total * BLOCK * heads * HD,
        total * width * 8,
        total * BLOCK * heads,
        grid=(heads, blocks),
        in_specs=[
            wide,
            narrow,
            table,
            table,
            pl.BlockSpec((BLOCK, 1), lambda h, b: (b, 0)),
            pl.BlockSpec((1, 1, BLOCK), lambda h, b: (b, 0, 0)),
        ],
        out_specs=[narrow, wide, pl.BlockSpec((8, 3 * HD), lambda h, b: (0, h))],
    )(
        joint,
        grad_mixture,
        cosine,
        sine,
        column,
        segments.reshape(blocks, 1, BLOCK),
    )


def result_kernel(where_ref, in_ref, got_ref, vec_ref, out_ref):
    width = in_ref.shape[1] // PIECES
    for r in range(PIECES):
        target = pl.ds(pl.multiple_of(where_ref[r] * width, width), width)
        at = slice(r * width, (r + 1) * width)
        total = got_ref[:, at].astype(F32) + in_ref[:, target].astype(F32) + vec_ref[4:5, at]
        out_ref[:, target] = total.astype(BF16)


def back_kernel(
    where_ref, in_ref, cot_ref, pad_ref, own_ref, below_ref, above_ref, out_ref, sum_ref
):
    x = in_ref[...].astype(F32)
    mean = jnp.mean(x, axis=1, keepdims=True)
    centred = x - mean
    inv = lax.rsqrt(jnp.mean(centred * centred, axis=1, keepdims=True) + EPS)
    features = x.shape[1]
    width = features // PIECES
    plain = jnp.zeros_like(mean)
    crossed = jnp.zeros_like(mean)
    for r in range(PIECES):
        target = pl.ds(pl.multiple_of(where_ref[r] * width, width), width)
        at = slice(r * width, (r + 1) * width)
        total = (
            own_ref[:, at].astype(F32)
            + below_ref[:, at].astype(F32)
            + above_ref[:, at].astype(F32)
        )
        sum_ref[:, at] = total
        plain += jnp.sum(total, axis=1, keepdims=True)
        normed = (in_ref[:, target].astype(F32) - mean) * inv
        crossed += jnp.sum(total * normed, axis=1, keepdims=True)
    plain = plain * (1.0 / features)
    crossed = crossed * (1.0 / features)
    marks = pad_ref[...].astype(F32)
    for r in range(PIECES):
        target = pl.ds(pl.multiple_of(where_ref[r] * width, width), width)
        at = slice(r * width, (r + 1) * width)
        normed = (in_ref[:, target].astype(F32) - mean) * inv
        seed = cot_ref[:, target].astype(F32) * marks
        out_ref[:, target] = (
            seed + inv * (sum_ref[:, at] - plain - normed * crossed)
        ).astype(BF16)


def finish(kernel, where, half, own_rows, got, tail, scratch=()):
    features = own_rows[0].shape[1]
    tile = got[0][1]
    row = (lambda at: at[PIECES]) if half is None else (lambda at: at[PIECES] * 2 + half)
    own = lambda w: pl.BlockSpec((tile, w), lambda i, at: (row(at), 0))
    here = lambda a: pl.BlockSpec(
        (tile, features), lambda i, at: (half if a.shape[0] > tile else 0, 0)
    )
    return call(
        kernel,
        shape(tile, features),
        20 * tile * features,
        12 * tile * features,
        grid_spec=pltpu.PrefetchScalarGridSpec(
            num_scalar_prefetch=1,
            grid=(1,),
            in_specs=[own(a.shape[1]) for a in own_rows]
            + [here(a) for a, _ in got]
            + [whole(*a.shape) for a in tail],
            out_specs=pl.BlockSpec((tile, features), lambda i, at: (0, 0)),
            scratch_shapes=[pltpu.VMEM((tile, features), F32)] * len(scratch),
        ),
    )(where, *own_rows, *(a for a, _ in got), *tail)


def swapped(a, bit):
    return lax.ppermute(a, "dp", [(i, i ^ bit) for i in range(PIECES)])


def crossed_over(from_x, from_y):
    core = lax.axis_index("dp") & 1
    pairs = [(i, i ^ (4 if i & 1 else 2)) for i in range(PIECES)]
    return lax.ppermute(jnp.where(core == 1, from_x, from_y), "dp", pairs)


def gather_pieces(items, after):
    gathered, arrived = {}, {}
    for name, own in items:
        if name in after:
            own, _ = lax.optimization_barrier((own, arrived[after[name]]))
        from_x = swapped(own, 2)
        from_y = swapped(own, 4)
        arrived[name] = (from_x, from_y)
        diagonal = crossed_over(from_x, from_y)
        near = (own, from_x, from_y, diagonal)
        far = [swapped(a, 1) for a in near]
        gathered[name] = [b for pair in zip(near, far) for b in pair]
    return gathered


def scattered_small(values):
    for bit in (4, 2, 1):
        values = values[:bit] + swapped(values[bit:], bit)
    return values[0]


def neighbours(t, spreading):
    n = lax.axis_size("mp")
    up = [(z, z + 1) for z in (range(t - 1, n - 1) if spreading else range(min(t, n - 1)))]
    return up, [(n - 1 - a, n - 1 - b) for a, b in up]


def leaving_kernel(at_ref, *refs):
    refs, outs = refs[:-2], refs[-2:]
    for i, out in enumerate(outs):
        rows = refs[i][...].astype(F32)
        if len(refs) > 2:
            rows = rows + refs[2 + i][...].astype(F32)
        out[...] = rows.astype(BF16)


def leaving(at, part, tile, got):
    features = part.shape[1]
    step = tile // 2
    own = lambda which: pl.BlockSpec((step, features), lambda i, at: (2 * at[which] + i, 0))
    here = pl.BlockSpec((step, features), lambda i, at: (i, 0))
    return call(
        leaving_kernel,
        [shape(tile, features)] * 2,
        2 * tile * features,
        (4 + 2 * len(got)) * tile * features * 2,
        grid_spec=pltpu.PrefetchScalarGridSpec(
            num_scalar_prefetch=1,
            grid=(2,),
            in_specs=[own(0), own(1)] + [here] * len(got),
            out_specs=[here] * 2,
        ),
    )(at, part, part, *got)


def summed_rows(part):
    n, me = lax.axis_size("mp"), lax.axis_index("mp")
    share = part.shape[0] // n
    tile = share // 2
    got = [(), ()]
    for t in range(1, n):
        up, down = neighbours(t, False)
        for half in (0, 1):
            blocks = jnp.stack([jnp.clip(n - t + me, 0, n - 1), jnp.clip(t + me - n, 0, n - 1)])
            at = 2 * blocks.astype(jnp.int32) + half
            going = leaving(at, part, tile, got[half])
            got[half] = (lax.ppermute(going[0], "mp", up), lax.ppermute(going[1], "mp", down))
    return got


def spread_rows(parts, room, late=None):
    n, me = lax.axis_size("mp"), lax.axis_index("mp")
    tile = parts[0].shape[0]
    rights, lefts = [parts], [parts]
    for t in range(1, n):
        up, down = neighbours(t, True)
        right, left = [], []
        for i in range(len(parts)):
            right.append(lax.ppermute(rights[-1][i], "mp", up))
            left.append(lax.ppermute(lefts[-1][i], "mp", down))
        rights.append(right)
        lefts.append(left)
    for t in [0] + list(range(2, n - 1)) + ([1, n - 1] if n > 2 else [1]):
        if t == 1 and late is not None:
            room, late = lax.optimization_barrier((room, late))
        for i in range(len(parts)):
            rows = parts[i] if t == 0 else lefts[t][i] + rights[n - t][i]
            at = (lax.rem(me + t, n) * len(parts) + i) * tile
            room = lax.dynamic_update_slice_in_dim(room, rows, at, 0)
    return room, late


def summed_over_mp(values):
    n = lax.axis_size("mp")
    if n & (n - 1):
        return lax.psum(values, "mp")
    bit = 1
    while bit < n:
        pairs = [(z, z ^ bit) for z in range(n)]
        values = values + lax.ppermute(values, "mp", pairs)
        bit *= 2
    return values


def step(
    inputs,
    segments,
    padding,
    first_gain,
    first_shift,
    second_gain,
    second_shift,
    joint_weight,
    joint_bias,
    dense_weight,
    dense_bias,
    expand_weight,
    expand_bias,
    reduce_weight,
    reduce_bias,
    cotangent,
):
    total, features = inputs.shape
    n_dp = lax.axis_size("dp")
    dp_at, mp_at = lax.axis_index("dp"), lax.axis_index("mp")
    order = jnp.arange(PIECES, dtype=jnp.int32)
    small = (
        joint_bias, expand_bias, first_gain, first_shift, second_gain, second_shift,
        dense_bias, reduce_bias,
    )
    longest = max(a.shape[0] for a in small)
    line = lax.broadcasted_iota(jnp.int32, (len(small), longest), 0)
    packed = jnp.zeros((len(small), longest), BF16)
    for i, a in enumerate(small):
        packed = jnp.where(line == i, jnp.pad(a, (0, longest - a.shape[0]))[None], packed)
    if n_dp == PIECES:
        order = dp_at ^ order
        packed = packed[None]
        packed = jnp.concatenate([packed, swapped(packed, 1)], axis=0)
        packed = jnp.concatenate([packed] + [swapped(packed, bit) for bit in (2, 4, 6)], axis=0)
        blocks = gather_pieces(
            (
                ("D", dense_weight),
                ("E", expand_weight),
                ("J", joint_weight),
                ("R", reduce_weight),
            ),
            {"R": "J"},
        )
        dense, joint_w, wide, reduce = (blocks[k] for k in "DJER")
        padding, segments, packed = lax.optimization_barrier((padding, segments, packed))
        by_device = jnp.take(packed, order, axis=0)
    else:
        packed = by_device = lax.all_gather(packed, "dp")
        rows = lambda a: jnp.split(lax.all_gather(a, "dp", axis=0, tiled=True), PIECES, 0)
        columns = lambda a: jnp.split(lax.all_gather(a, "dp", axis=1, tiled=True), PIECES, 1)
        dense, joint_w = columns(dense_weight), rows(joint_weight)
        wide, reduce = rows(expand_weight), columns(reduce_weight)
    where = jnp.concatenate([order, mp_at[None].astype(jnp.int32)])
    taken = lambda a, i: a[:, i, : small[i].shape[0]].reshape(1, -1).astype(F32)
    bias_j, bias_e = taken(by_device, 0), taken(by_device, 1)
    vectors = jnp.concatenate(
        [taken(packed, i) for i in range(2, 6)]
        + [taken(packed, 6) + taken(packed, 7), jnp.zeros((3, features), F32)]
    )

    marks = padding[:, None]
    hidden_one, hidden_two, normed, seed, bias_back = rows_pass(
        where, inputs, cotangent, marks, vectors
    )
    cosine, sine = rotary_tables(segments)
    column = segments.reshape(total, 1)
    cosine, sine, column, seed = lax.optimization_barrier((cosine, sine, column, seed))

    grad_mixture = mixture_back(seed, dense)
    joint = project(hidden_one, joint_w, bias_j)
    mixture, joint_low, joint_bias_back = attend(joint, grad_mixture, cosine, sine, column, segments)
    activated, slope = expand(hidden_two, wide, bias_e)
    branch = branch_of(mixture, activated, dense, reduce)
    before_low, expand_bias_back = before_back(seed, reduce, slope)
    gx, gains = gx_of(joint_low, before_low, normed, vectors, joint_w, wide)

    tile = total // lax.axis_size("mp") // 2
    branches = lax.psum_scatter(branch, "mp", scatter_dimension=0, tiled=True)
    result = finish(
        result_kernel, where, None, (inputs,), ((branches, 2 * tile),),
        (vectors,),
    )
    result, _ = spread_rows([result], branch)
    grads = gradient(
        where, (hidden_one, seed, hidden_two, seed),
        (joint_low, mixture, before_low, activated),
    )
    grads, _ = lax.optimization_barrier((grads, branches))
    grads = lax.psum_scatter(grads, "dp", scatter_dimension=0, tiled=True)
    widths = [a.shape[1] for a in (joint_low, mixture, before_low, activated)]
    weights = unpack(grads, widths)

    back = [
        finish(back_kernel, where, half, (inputs, cotangent, marks, gx),
              tuple((a, tile) for a in got), (), (0,))
        for half, got in enumerate(summed_rows(gx))
    ]
    back, weights = spread_rows(back, normed, weights)

    gains = jnp.sum(gains.reshape(4, 8, features), axis=1)
    gains = summed_over_mp(gains)
    straight = jnp.concatenate([gains, jnp.sum(bias_back, axis=0)[None]])
    by_row = [
        jnp.sum(joint_bias_back, axis=0).reshape(n_dp, -1),
        jnp.sum(expand_bias_back, axis=0).reshape(n_dp, -1),
    ]
    if n_dp == PIECES:
        by_row = [jnp.take(a, order, axis=0) for a in by_row]
    sums = jnp.concatenate(
        by_row + [straight[i].reshape(n_dp, -1) for i in range(5)], axis=1
    )
    if n_dp == PIECES:
        sums = scattered_small(sums)
    else:
        sums = lax.psum_scatter(sums, "dp", scatter_dimension=0, tiled=True).reshape(-1)
    widths = [joint_bias.shape[0], expand_bias.shape[0]] + [features // n_dp] * 5
    cuts = [sum(widths[:i]) for i in range(len(widths) + 1)]
    parts = [sums[a:b] for a, b in zip(cuts, cuts[1:])]
    return (
        result, back, parts[2], parts[3], parts[4], parts[5],
        weights[0], parts[0], weights[1], parts[6],
        weights[2], parts[1], weights[3], parts[6],
    )


def solution(mesh):
    placed = (
        P("dp", None), P("dp"), P("dp"), P("dp"), P("dp"), P("dp"), P("dp"),
        P("dp", "mp"), P(("mp", "dp")), P("mp", "dp"), P("dp"),
        P("dp", "mp"), P(("mp", "dp")), P("mp", "dp"), P("dp"), P("dp", None),
    )
    return jax.shard_map(
        step,
        mesh=mesh,
        in_specs=placed,
        out_specs=(
            P("dp", None), P("dp", None), P("dp"), P("dp"), P("dp"), P("dp"),
            P("dp", "mp"), P(("mp", "dp")), P("mp", "dp"), P("dp"),
            P("dp", "mp"), P(("mp", "dp")), P("mp", "dp"), P("dp"),
        ),
        check_vma=False,
    )
```
